32 devices in a mesh: section: 2 (over y), dp: 16 (over z, x, core).
Axes of the slice: x: 2, y: 2, z: 4, core: 2. Of those that a mesh axis runs over, the one named last changes fastest.
Arguments:
- activations: bfloat16 [2, 2048, 8192], P('section', 'dp'), may hold values from -6 to 6
- cotangent: bfloat16 [2048, 8192], P('dp'), may hold values from -6 to 6
- token_ids: int32 [2048], P('dp'), may hold values from 0 to 30527, as said below
- gains: float32 [2, 8192], P('section'), may hold values from 0.1 to 1.9
- factors: bfloat16 [2, 4, 64, 128, 128], P('section'), may hold values from -0.5 to 0.5
- monarch_perm: int32 [2, 8192], P('section'), may hold values from 0 to 8191, each once within a row
Outputs:
- grad_acts: bfloat16 [2, 2048, 8192], P('section', 'dp')
- factor_grads: float32 [2, 4, 64, 128, 128], P('section', None, 'dp')
- gain_grads: float32 [2, 8192], P('section', 'dp')
The draws below stay inside these ranges and needn't reach their ends.
Inputs may be any that keep to these rules, and one draw needn't show every extreme that they name: `token_ids`: 0 marks padding; in each device's block of 128 tokens the padding is a tail, possibly empty, of at most three quarters of the block; other ids lie in 1 to 30527. `monarch_perm`: each row is a permutation of 0 to 8191.
All inputs are finite; a program needn't handle non-finite values.
Results may differ from the reference program's by a relative error of at most 0.01.
Values may be sent and summed in bfloat16 or wider, within the bound.
No kernel may reach another device: no remote copies, remote signals or barrier semaphores. Data moves between devices by JAX's collectives and lax.ppermute only.
A program may use at most 192 MiB of HBM per device.

```python
import jax
import jax.numpy as jnp
from jax import lax

NB = 64
BS = 128
VOCAB = 30528
TOK_DEV = 128
D = 8192
SECTIONS = 2
TOKENS = 2048
N_DP = 16


def draw_token_ids(key, part):
    key_ids = jax.random.fold_in(key, 11)
    key_tail = jax.random.fold_in(key, 23)
    blocks = TOKENS // TOK_DEV
    values = jax.random.randint(key_ids, (blocks, TOK_DEV), 1, VOCAB)
    position = jnp.arange(TOK_DEV, dtype=jnp.int32)[None, :]
    block_index = jnp.arange(blocks, dtype=jnp.int32)[:, None]
    values = jnp.where(jnp.logical_and(block_index == 0, position == 0), VOCAB - 1, values)
    start = jax.random.randint(key_tail, (blocks, 1), TOK_DEV // 4, TOK_DEV + 1)
    start = jnp.where(block_index == 0, jnp.minimum(start, TOK_DEV - 1), start)
    return jnp.where(position < start, values, 0).reshape(TOKENS).astype(jnp.int32)


def with_spikes(entries, own_key, source, target, parts, factor):
    def block_of(axis_at):
        return (jnp.arange(entries.shape[axis_at]) // (entries.shape[axis_at] // parts)).reshape((-1,) + (1,) * (entries.ndim - 1 - axis_at))

    near = jax.random.permutation(own_key, parts)[block_of(target)]
    far = (block_of(target) + parts // 2) % parts
    return jnp.where((block_of(source) == near) | (block_of(source) == far), factor * entries, entries)


def block_levels(stream_key, dims, cuts, least, largest):
    def one(dim, parts):
        steps = jax.random.uniform(jax.random.fold_in(jax.random.fold_in(stream_key, 6), dim), (parts,), jnp.float32, least / len(cuts), largest / len(cuts))
        return jnp.repeat(jnp.exp(steps), dims[dim] // parts).reshape((-1,) + (1,) * (len(dims) - dim - 1))

    factor_of = one(*cuts[0])
    for cut in cuts[1:]:
        factor_of = factor_of * one(*cut)
    return factor_of


def scatter_about(key, extent, deviation, limit, cuts=(), kind=jnp.bfloat16):
    array = jax.random.normal(key, extent, jnp.float32) * deviation
    if len(cuts) > 0:
        array = block_levels(key, extent, cuts, -0.22, 0.18) * array
    return jnp.clip(array, min=-limit, max=limit).astype(kind)


def bell_draw_with(rng, shape, deviation, limit, cuts, heavy, held_as=jnp.bfloat16):
    drawn = deviation * jax.random.normal(rng, shape, jnp.float32)
    if cuts:
        drawn = drawn * block_levels(rng, shape, cuts, -0.22, 0.18)
    return jnp.clip(with_spikes(drawn, jax.random.fold_in(rng, 3), *heavy), -limit, limit).astype(held_as)


def setup_inputs(seed: int = 0) -> dict:
    arg_keys = jax.random.split(jax.random.key(seed), 7)
    activations = bell_draw_with(arg_keys[0], (SECTIONS, TOKENS, D), 1.0, 6.0, ((0, 2), (1, 16)), (1, 2, 16, 2.0))
    cotangent = bell_draw_with(arg_keys[1], (TOKENS, D), 1.0, 6.0, ((0, 16),), (0, 1, 16, 2.0))
    token_ids = draw_token_ids(jax.random.fold_in(arg_keys[6], 71), 0)
    gains = jnp.clip(1.0 + 0.18 * jax.random.normal(arg_keys[3], (SECTIONS, D), jnp.float32), 0.1, 1.9)
    factors = scatter_about(arg_keys[4], (SECTIONS, 4, NB, BS, BS), BS ** -0.5, 0.5, ((0, 2),))
    monarch_perm = jax.vmap(lambda own: jax.random.permutation(own, D))(jax.random.split(arg_keys[5], SECTIONS)).reshape((SECTIONS, D)).astype(jnp.int32)
    return {"activations": activations, "cotangent": cotangent, "token_ids": token_ids, "gains": gains, "factors": factors, "monarch_perm": monarch_perm}


inv_sqrt_two = 0.7071067811865476
inv_sqrt_two_pi = 0.3989422804014327

def block_mul(rows, factor):
    split = rows.astype(jnp.float32).reshape(rows.shape[0], factor.shape[0], factor.shape[1])
    out = jnp.einsum('rki,kij->rkj', split, factor.astype(jnp.float32), precision=lax.Precision.HIGHEST)
    return out.reshape(rows.shape[0], rows.shape[1])

def block_mul_t(rows, factor):
    split = rows.astype(jnp.float32).reshape(rows.shape[0], factor.shape[0], factor.shape[1])
    out = jnp.einsum('rkj,kij->rki', split, factor.astype(jnp.float32), precision=lax.Precision.HIGHEST)
    return out.reshape(rows.shape[0], rows.shape[1])

def block_grad(left, right, blocks, size):
    lsplit = left.astype(jnp.float32).reshape(left.shape[0], blocks, size)
    rsplit = right.astype(jnp.float32).reshape(right.shape[0], blocks, size)
    return jnp.einsum('rki,rkj->kij', lsplit, rsplit, precision=lax.Precision.HIGHEST)

def section_backward(x, grad_out, gamma, factor, perm, inverse):
    blocks, size = (factor.shape[1], factor.shape[2])
    xf = x.astype(jnp.float32)
    scale = lax.rsqrt(lax.optimization_barrier(jnp.mean(xf * xf, axis=1, keepdims=True)) + 1e-06)
    zed = xf * scale
    normed = (zed * gamma).astype(jnp.bfloat16)
    first = block_mul(normed, factor[0]).astype(jnp.bfloat16)
    first_p = jnp.take(first, perm, axis=1)
    pre = block_mul(first_p, factor[1])
    cdf = 0.5 * (1.0 + jax.scipy.special.erf(pre * inv_sqrt_two))
    hidden = (pre * cdf).astype(jnp.bfloat16)
    second = block_mul(hidden, factor[2]).astype(jnp.bfloat16)
    second_p = jnp.take(second, perm, axis=1)
    grad_three = block_grad(second_p, grad_out, blocks, size)
    grad_sp = block_mul_t(grad_out, factor[3]).astype(jnp.bfloat16)
    grad_second = jnp.take(grad_sp, inverse, axis=1)
    grad_two = block_grad(hidden, grad_second, blocks, size)
    grad_hidden = block_mul_t(grad_second, factor[2])
    slope = cdf + pre * jnp.exp(-0.5 * pre * pre) * inv_sqrt_two_pi
    grad_pre = (grad_hidden * slope).astype(jnp.bfloat16)
    grad_one = block_grad(first_p, grad_pre, blocks, size)
    grad_fp = block_mul_t(grad_pre, factor[1]).astype(jnp.bfloat16)
    grad_first = jnp.take(grad_fp, inverse, axis=1)
    grad_zero = block_grad(normed, grad_first, blocks, size)
    grad_normed = block_mul_t(grad_first, factor[0])
    grad_gamma = lax.optimization_barrier(jnp.sum(grad_normed * zed, axis=0))
    grad_zed = grad_normed * gamma
    inner = lax.optimization_barrier(jnp.mean(grad_zed * zed, axis=1, keepdims=True))
    grad_x = (grad_out.astype(jnp.float32) + scale * (grad_zed - zed * inner)).astype(jnp.bfloat16)
    return (grad_x, jnp.stack([grad_zero, grad_one, grad_two, grad_three]), grad_gamma)

def reference(activations, cotangent, token_ids, gains, factors, monarch_perm):
    live = (token_ids != 0).astype(jnp.bfloat16)
    incoming = cotangent * live[:, None]
    acts_list = [None] * SECTIONS
    fgrad_list = [None] * SECTIONS
    ggrad_list = [None] * SECTIONS
    for section in reversed(range(SECTIONS)):
        perm = monarch_perm[section].astype(jnp.int32)
        inverse = jnp.zeros((D,), jnp.int32).at[perm].set(jnp.arange(D, dtype=jnp.int32))
        x_blocks = activations[section].reshape(N_DP, TOK_DEV, D)
        g_blocks = incoming.reshape(N_DP, TOK_DEV, D)
        gamma = gains[section]
        factor = factors[section]

        def step(carry, pair):
            grad_x, grads, grad_gamma = section_backward(pair[0], pair[1], gamma, factor, perm, inverse)
            return ((carry[0] + grads, carry[1] + grad_gamma), grad_x)
        init = (jnp.zeros((4, NB, BS, BS), jnp.float32), jnp.zeros((D,), jnp.float32))
        (grads, grad_gamma), grad_x = lax.scan(step, init, (x_blocks, g_blocks))
        acts_list[section] = grad_x.reshape(TOKENS, D)
        fgrad_list[section] = grads / N_DP
        ggrad_list[section] = grad_gamma / N_DP
        incoming = acts_list[section]
    return (jnp.stack(acts_list), jnp.stack(fgrad_list), jnp.stack(ggrad_list))
```

```python
import functools

import jax
import jax.numpy as jnp
from jax import lax
from jax.experimental import pallas as pl
from jax.experimental.pallas import tpu as pltpu
from jax.sharding import PartitionSpec as P

F32 = jnp.float32
BF16 = jnp.bfloat16
inv_sqrt_two = 0.7071067811865476
inv_sqrt_two_pi = 0.3989422804014327
STEP = 8
VMEM_BYTES = 44 << 20


def dot(a, b, ca, cb):
    return lax.dot_general(a, b, (((ca,), (cb,)), ((), ())), preferred_element_type=F32)


def whole(*shape):
    return pl.BlockSpec(shape, lambda *_: (0,) * len(shape))


def call(body, name, grid, in_specs, out_specs, out_shape, scratch=(), prefetch=1):
    return pl.pallas_call(
        body,
        name=name,
        out_shape=out_shape,
        grid_spec=pltpu.PrefetchScalarGridSpec(
            num_scalar_prefetch=prefetch,
            grid=grid,
            in_specs=in_specs,
            out_specs=out_specs,
            scratch_shapes=scratch,
        ),
        compiler_params=pltpu.CompilerParams(vmem_limit_bytes=VMEM_BYTES),
    )


def rounded(v):
    return v.astype(BF16).astype(F32)


def normed_block(x, scale, gamma, cols):
    return (x[:, cols].astype(F32) * scale[...] * gamma[:, cols]).astype(BF16)


def gather_rows(perm, base, source, target, count):
    for i in range(count):
        target[pl.ds(i, 1), :] = source[pl.ds(perm[base + i], 1), :]


def scatter_rows(perm, base, source, target, count):
    for i in range(count):
        target[pl.ds(perm[base + i], 1), :] = source[pl.ds(i, 1), :]


def forward_first(perm, x, gamma, fac, ap_t, h_t, slope_t, scale, a_t, rows):
    phase, c = pl.program_id(0), pl.program_id(1)
    bs = fac.shape[2]
    blocks = x.shape[1] // bs

    @pl.when(jnp.logical_and(phase == 0, c == 0))
    def _():
        def add(k, acc):
            xk = x[:, pl.ds(pl.multiple_of(k * bs, bs), bs)].astype(F32)
            return acc + xk * xk

        acc = lax.fori_loop(0, blocks, add, jnp.zeros((x.shape[0], bs), F32), unroll=8)
        mean = jnp.sum(acc, axis=1, keepdims=True) / x.shape[1]
        scale[...] = jnp.broadcast_to(lax.rsqrt(mean + 1e-06), scale.shape)

    @pl.when(phase == 0)
    def _():
        for k in range(STEP):
            at = pl.multiple_of((c * STEP + k) * bs, bs)
            n = normed_block(x, scale, gamma, pl.ds(at, bs))
            a_t[pl.ds(at, bs), :] = rounded(dot(fac[0, k], n, 0, 1))

    @pl.when(phase == 1)
    def _():
        for k in range(STEP):
            at = pl.multiple_of((c * STEP + k) * bs, bs)
            gather_rows(perm, at, a_t, rows.at[k], bs)
            ap = rows[k].astype(BF16)
            ap_t[pl.ds(k * bs, bs), :] = ap
            pre = dot(fac[0, k], ap, 0, 0)
            cdf = 0.5 * (1.0 + lax.erf(pre * inv_sqrt_two))
            h_t[pl.ds(k * bs, bs), :] = (pre * cdf).astype(BF16)
            slope_t[pl.ds(k * bs, bs), :] = cdf + pre * jnp.exp(-0.5 * pre * pre) * inv_sqrt_two_pi


def forward_second(perm, h_t, fac, cp_t, c_t, rows):
    phase, c = pl.program_id(0), pl.program_id(1)
    bs = fac.shape[2]

    @pl.when(phase == 0)
    def _():
        for k in range(STEP):
            at = pl.multiple_of((c * STEP + k) * bs, bs)
            c_t[pl.ds(at, bs), :] = rounded(dot(fac[0, k], h_t[pl.ds(k * bs, bs), :], 0, 0))

    @pl.when(phase == 1)
    def _():
        for k in range(STEP):
            at = pl.multiple_of((c * STEP + k) * bs, bs)
            gather_rows(perm, at, c_t, rows.at[k], bs)
            cp_t[pl.ds(k * bs, bs), :] = rows[k].astype(BF16)


def backward_data(perm, cot, live, slope_t, fac, fac_one, x, scale, gamma, grad_x, gc_t, ga_t, gn, rows):
    phase, c = pl.program_id(0), pl.program_id(1)
    bs = fac.shape[2]
    blocks = x.shape[1] // bs

    def gy_block(cols):
        return (cot[:, cols].astype(F32) * live[...]).astype(BF16)

    @pl.when(phase == 0)
    def _():
        for k in range(STEP):
            at = pl.multiple_of((c * STEP + k) * bs, bs)
            rows[k] = rounded(dot(fac[0, k], gy_block(pl.ds(at, bs)), 1, 1))
            scatter_rows(perm, at, rows.at[k], gc_t, bs)

    @pl.when(phase == 1)
    def _():
        for k in range(STEP):
            at = pl.multiple_of((c * STEP + k) * bs, bs)
            gh = dot(fac[0, k], gc_t[pl.ds(at, bs), :].astype(BF16), 1, 0)
            gpre = (gh * slope_t[pl.ds(k * bs, bs), :]).astype(BF16)
            rows[k] = rounded(dot(fac_one[0, k], gpre, 1, 0))
            scatter_rows(perm, at, rows.at[k], ga_t, bs)

    @pl.when(phase == 2)
    def _():
        for k in range(STEP):
            at = pl.multiple_of((c * STEP + k) * bs, bs)
            gn[:, pl.ds(at, bs)] = dot(ga_t[pl.ds(at, bs), :].astype(BF16), fac[0, k], 0, 1)

    @pl.when(jnp.logical_and(phase == 2, c == pl.num_programs(1) - 1))
    def _():
        finish(lambda cols: gy_block(cols), x, scale, gamma, gn, grad_x, blocks, bs)


def finish(gy_block, x, scale, gamma, gn, grad_x, blocks, bs):
    def add(k, acc):
        cols = pl.ds(pl.multiple_of(k * bs, bs), bs)
        z = x[:, cols].astype(F32) * scale[...]
        return acc + gn[:, cols] * gamma[:, cols] * z

    acc = lax.fori_loop(0, blocks, add, jnp.zeros((x.shape[0], bs), F32), unroll=8)
    inner = jnp.broadcast_to(jnp.sum(acc, axis=1, keepdims=True) / x.shape[1], acc.shape)

    def emit(k, _):
        cols = pl.ds(pl.multiple_of(k * bs, bs), bs)
        z = x[:, cols].astype(F32) * scale[...]
        grad = gy_block(cols).astype(F32) + scale[...] * (gn[:, cols] * gamma[:, cols] - z * inner)
        grad_x[:, cols] = grad.astype(BF16)
        return 0

    lax.fori_loop(0, blocks, emit, 0, unroll=4)


def split_blocks(flags, own):
    for k in range(STEP // 2):
        group, within = divmod(k, own)
        base = group * 2 * own + within
        yield k, base + flags[0] * own, base + (1 - flags[0]) * own


def chosen_gy(flags, cot, live, moved, cols):
    seeded = (cot[:, cols].astype(F32) * live[...]).astype(BF16)
    return jnp.where(flags[1] == 1, seeded, moved[:, cols])


def backward_three(own, perm, flags, cot, live, moved, cp_t, fac, keep, send, gc_out, gc_t, rows):
    c = pl.program_id(0)
    bs = fac.shape[2]

    def gy_block(k):
        return chosen_gy(flags, cot, live, moved, pl.ds(pl.multiple_of((c * STEP + k) * bs, bs), bs))

    for k in range(STEP):
        rows[k] = rounded(dot(fac[0, k], gy_block(k), 1, 1))
        scatter_rows(perm, pl.multiple_of((c * STEP + k) * bs, bs), rows.at[k], gc_t, bs)
    for k, stays, goes in split_blocks(flags, own):
        for out, block in ((keep, stays), (send, goes)):
            left = cp_t[pl.ds(pl.multiple_of(block * bs, bs), bs), :]
            out[k] = dot(left, gy_block(block), 1, 0).astype(BF16)

    @pl.when(c == pl.num_programs(0) - 1)
    def _():
        gc_out[...] = gc_t[...].astype(BF16)


def backward_two_one(own, perm, flags, gc_t, h_t, ap_t, slope_t, fac_two, fac_one, keep_two, send_two, keep_one, send_one, ga_out, ga_t, gpre, rows):
    c = pl.program_id(0)
    bs = fac_two.shape[2]
    for k in range(STEP):
        here = pl.ds(k * bs, bs)
        gh = dot(fac_two[0, k], gc_t[here, :], 1, 0)
        gpre[here, :] = (gh * slope_t[here, :]).astype(BF16)
        rows[k] = rounded(dot(fac_one[0, k], gpre[here, :], 1, 0))
        scatter_rows(perm, pl.multiple_of((c * STEP + k) * bs, bs), rows.at[k], ga_t, bs)
    for k, stays, goes in split_blocks(flags, own):
        for two, one, block in ((keep_two, keep_one, stays), (send_two, send_one, goes)):
            at = pl.ds(pl.multiple_of(block * bs, bs), bs)
            two[k] = dot(h_t[at, :], gc_t[at, :], 1, 1).astype(BF16)
            one[k] = dot(ap_t[at, :], gpre[at, :], 1, 1).astype(BF16)

    @pl.when(c == pl.num_programs(0) - 1)
    def _():
        ga_out[...] = ga_t[...].astype(BF16)


def backward_zero(own, flags, ga_t, x, scale, gamma, keep, send):
    c = pl.program_id(0)
    bs = x.shape[1] // (pl.num_programs(0) * STEP)
    for k, stays, goes in split_blocks(flags, own):
        for out, block in ((keep, stays), (send, goes)):
            at = pl.multiple_of(block * bs, bs)
            n = normed_block(x, scale, gamma, pl.ds(pl.multiple_of(c * STEP * bs + at, bs), bs))
            out[k] = dot(ga_t[pl.ds(at, bs), :], n, 1, 0).astype(BF16)


def backward_last(flags, ga_t, cot, live, moved, x, scale, gamma, fac, grad_x, grad_gamma, gn):
    c = pl.program_id(0)
    bs = fac.shape[2]
    blocks = x.shape[1] // bs
    for k in range(STEP):
        cols = pl.ds(pl.multiple_of((c * STEP + k) * bs, bs), bs)
        value = dot(ga_t[pl.ds(k * bs, bs), :], fac[0, k], 0, 1)
        gn[:, cols] = value
        z = x[:, cols].astype(F32) * scale[...]
        grad_gamma[:, pl.ds(k * bs, bs)] = jnp.sum(value * z, axis=0, keepdims=True)

    @pl.when(c == pl.num_programs(0) - 1)
    def _():
        finish(lambda cols: chosen_gy(flags, cot, live, moved, cols), x, scale, gamma, gn, grad_x, blocks, bs)


def halved(keep, send, stage, own, me, replicas):
    came = lax.ppermute(send, "dp", [(i, i ^ (1 << stage)) for i in range(replicas)])
    if (2 << stage) == replicas:
        return keep.astype(F32) + came.astype(F32), None
    split = (keep.shape[0] // (2 * own), 2, own) + keep.shape[1:]
    bit = (me >> (stage + 1)) & 1

    def part(which):
        a = lax.dynamic_index_in_dim(keep.reshape(split), which, 1, keepdims=False)
        b = lax.dynamic_index_in_dim(came.reshape(split), which, 1, keepdims=False)
        total = (a.astype(F32) + b.astype(F32)).astype(keep.dtype)
        return total.reshape((split[0] * own,) + keep.shape[1:])

    return part(bit), part(1 - bit)


def summed(keep, send, own, me, replicas):
    for stage in range(replicas.bit_length() - 1):
        keep, send = halved(keep, send, stage, own, me, replicas)
    return keep / replicas


def on_device(replicas, sections, activations, cotangent, token_ids, gains, factors, monarch_perm):
    x = activations[0]
    gamma = gains
    fac = factors[0]
    perm = monarch_perm[0]
    tokens, width = x.shape
    blocks, bs = fac.shape[1], fac.shape[2]
    own = blocks // replicas
    steps = blocks // STEP
    here = lax.axis_index("section")
    me = lax.axis_index("dp")
    live = jnp.broadcast_to((token_ids != 0).astype(F32)[:, None], (tokens, bs))
    flags = jnp.stack([me & 1, (here == sections - 1).astype(jnp.int32)])

    tok = whole(tokens, width)
    sca = whole(tokens, bs)
    gam = whole(1, width)
    chunk = (STEP * bs, tokens)
    fblock = (1, STEP, bs, bs)
    f_at = lambda which: pl.BlockSpec(fblock, lambda c, *_: (which, c, 0, 0))
    c_at = pl.BlockSpec(chunk, lambda c, *_: (c, 0))
    feat = lambda dt: jax.ShapeDtypeStruct((width, tokens), dt)
    half = jax.ShapeDtypeStruct((blocks // 2, bs, bs), BF16)
    half_at = pl.BlockSpec((STEP // 2, bs, bs), lambda c, *_: (c, 0, 0))
    big = pltpu.VMEM((width, tokens), F32)
    rows = pltpu.VMEM((STEP, bs, tokens), F32)
    late = pl.BlockSpec(chunk, lambda ph, c, *_: (ph * c, 0))

    ap_t, h_t, slope_t, scale = call(
        forward_first,
        "forward_first",
        (2, steps),
        [tok, gam, pl.BlockSpec(fblock, lambda ph, c, *_: (ph, c, 0, 0))],
        [late, late, late, sca],
        [feat(BF16), feat(BF16), feat(F32), jax.ShapeDtypeStruct((tokens, bs), F32)],
        [big, rows],
    )(perm, x, gamma, fac)

    which = lambda ph: jnp.where(ph == 0, 3, jnp.where(ph == 1, 2, 0))
    mid = lambda ph, c: jnp.where(ph == 0, 0, jnp.where(ph == 1, c, steps - 1))
    grad_x = call(
        backward_data,
        "backward_data",
        (3, steps),
        [
            tok,
            sca,
            pl.BlockSpec(chunk, lambda ph, c, *_: (mid(ph, c), 0)),
            pl.BlockSpec(fblock, lambda ph, c, *_: (which(ph), c, 0, 0)),
            pl.BlockSpec(fblock, lambda ph, c, *_: (1, mid(ph, c), 0, 0)),
            tok,
            sca,
            gam,
        ],
        tok,
        jax.ShapeDtypeStruct((tokens, width), BF16),
        [big, big, pltpu.VMEM((tokens, width), F32), rows],
    )(perm, cotangent, live, slope_t, fac, fac, x, scale, gamma)
    moved = lax.ppermute(grad_x, "section", [(i, i - 1) for i in range(1, sections)])

    cp_t = call(
        forward_second,
        "forward_second",
        (2, steps),
        [
            pl.BlockSpec(chunk, lambda ph, c, *_: (jnp.where(ph == 0, c, steps - 1), 0)),
            pl.BlockSpec(fblock, lambda ph, c, *_: (2, jnp.where(ph == 0, c, steps - 1), 0, 0)),
        ],
        late,
        feat(BF16),
        [big, rows],
    )(perm, h_t, fac)

    keep_three, send_three, gc_t = call(
        functools.partial(backward_three, own),
        "backward_three",
        (steps,),
        [tok, sca, tok, c_at, f_at(3)],
        [half_at, half_at, whole(width, tokens)],
        [half, half, feat(BF16)],
        [big, rows],
        prefetch=2,
    )(perm, flags, cotangent, live, moved, cp_t, fac)
    keep_two, send_two, keep_one, send_one, ga_t = call(
        functools.partial(backward_two_one, own),
        "backward_two_one",
        (steps,),
        [c_at, c_at, c_at, c_at, f_at(2), f_at(1)],
        [half_at] * 4 + [whole(width, tokens)],
        [half] * 4 + [feat(BF16)],
        [big, pltpu.VMEM(chunk, BF16), rows],
        prefetch=2,
    )(perm, flags, gc_t, h_t, ap_t, slope_t, fac, fac)
    keep_zero, send_zero = call(
        functools.partial(backward_zero, own),
        "backward_zero",
        (steps,),
        [c_at, tok, sca, gam],
        [half_at, half_at],
        [half, half],
    )(flags, ga_t, x, scale, gamma)
    out_grad, grad_gamma = call(
        backward_last,
        "backward_last",
        (steps,),
        [c_at, tok, sca, tok, tok, sca, gam, f_at(0)],
        [tok, pl.BlockSpec((1, STEP * bs), lambda c, *_: (0, c))],
        [jax.ShapeDtypeStruct((tokens, width), BF16), jax.ShapeDtypeStruct((1, width), F32)],
        [pltpu.VMEM((tokens, width), F32)],
    )(flags, ga_t, cotangent, live, moved, x, scale, gamma, fac)

    total = [
        summed(keep, send, own, me, replicas)
        for keep, send in ((keep_zero, send_zero), (keep_one, send_one), (keep_two, send_two), (keep_three, send_three))
    ]
    total[0] = jnp.swapaxes(total[0], 1, 2)
    pieces = grad_gamma.reshape(replicas // 2, 2, width // replicas)
    gamma_keep = lax.dynamic_index_in_dim(pieces, me & 1, 1, keepdims=False)
    gamma_send = lax.dynamic_index_in_dim(pieces, 1 - (me & 1), 1, keepdims=False)
    gamma_total = summed(gamma_keep, gamma_send, 1, me, replicas)
    return (out_grad[None], jnp.stack(total)[None], gamma_total)


def solution(mesh):
    replicas, sections = mesh.shape["dp"], mesh.shape["section"]
    in_specs = (
        P("section", "dp", None),
        P("dp", None),
        P("dp"),
        P("section", None),
        P("section", None, None, None, None),
        P("section", None),
    )
    out_specs = (P("section", "dp", None), P("section", None, "dp", None, None), P("section", "dp"))
    return jax.shard_map(
        functools.partial(on_device, replicas, sections),
        mesh=mesh,
        in_specs=in_specs,
        out_specs=out_specs,
        check_vma=False,
    )
```

```python
import functools

import jax
import jax.numpy as jnp
from jax import lax
from jax.experimental import pallas as pl
from jax.experimental.pallas import tpu as pltpu
from jax.sharding import PartitionSpec as P

F32 = jnp.float32
BF16 = jnp.bfloat16
inv_sqrt_two = 0.7071067811865476
inv_sqrt_two_pi = 0.3989422804014327
STEP = 16
UNROLL = 8
EXTRA = 16
VMEM_BYTES = 56 << 20


def dot(a, b, ca, cb):
    return lax.dot_general(a, b, (((ca,), (cb,)), ((), ())), preferred_element_type=F32)


def whole(*shape):
    return pl.BlockSpec(shape, lambda *_: (0,) * len(shape))


def call(body, name, grid, in_specs, out_specs, out_shape, scratch=(), prefetch=1):
    return pl.pallas_call(
        body,
        name=name,
        out_shape=out_shape,
        grid_spec=pltpu.PrefetchScalarGridSpec(
            num_scalar_prefetch=prefetch,
            grid=grid,
            in_specs=in_specs,
            out_specs=out_specs,
            scratch_shapes=scratch,
        ),
        compiler_params=pltpu.CompilerParams(vmem_limit_bytes=VMEM_BYTES),
    )


def each_block(body, count=STEP, unroll=UNROLL):
    def some(i, carry):
        for u in range(unroll):
            body(i * unroll + u, u)
        return carry

    lax.fori_loop(0, count // unroll, some, 0)


def at_block(k, bs):
    return pl.ds(pl.multiple_of(k * bs, bs), bs)


def rounded(v):
    return v.astype(BF16).astype(F32)


def zed_block(x, scale, cols):
    return x[:, cols].astype(F32) * scale[...]


def gather_rows(perm, base, source, target, count):
    for i in range(count):
        target[pl.ds(i, 1), :] = source[pl.ds(perm[base + i], 1), :]


def scatter_rows(perm, base, source, target, count):
    for i in range(count):
        target[pl.ds(perm[base + i], 1), :] = source[pl.ds(i, 1), :]


def seeded_block(cot, live, cols):
    return (cot[:, cols].astype(F32) * live[...]).astype(BF16)


def gradient(gy, gn, gamma, z, scale, inner):
    return (gy.astype(F32) + scale[...] * (gn * gamma - z * inner[...])).astype(BF16)


def first_pass(perm, x, cot, live, gamma, fac_a, fac_b, ap_t, h_t, slope_t, scale, grad_x, a_t, gc_t, ga_t, gn, acc, rows, rows_b):
    phase, c = pl.program_id(0), pl.program_id(1)
    bs = fac_a.shape[2]
    blocks = x.shape[1] // bs

    @pl.when(jnp.logical_and(phase == 0, c == 0))
    def _():
        def add(k, total):
            xk = x[:, at_block(k, bs)].astype(F32)
            return total + xk * xk

        total = lax.fori_loop(0, blocks, add, jnp.zeros((x.shape[0], bs), F32), unroll=8)
        mean = jnp.sum(total, axis=1, keepdims=True) / x.shape[1]
        scale[...] = jnp.broadcast_to(lax.rsqrt(mean + 1e-06), scale.shape)
        acc[...] = jnp.zeros(acc.shape, F32)

    @pl.when(phase == 0)
    def _():
        def one(k, u):
            block = c * STEP + k
            cols = at_block(block, bs)
            n = (zed_block(x, scale, cols) * gamma[:, cols]).astype(BF16)
            a_t[cols, :] = rounded(dot(fac_a[0, k], n, 0, 1))
            rows[u] = rounded(dot(fac_b[0, k], seeded_block(cot, live, at_block(k, bs)), 1, 1))
            scatter_rows(perm, block * bs, rows.at[u], gc_t, bs)

        each_block(one)

    @pl.when(phase == 1)
    def _():
        def one(k, u):
            block = c * STEP + k
            here = at_block(k, bs)
            gather_rows(perm, block * bs, a_t, rows.at[u], bs)
            ap = rows[u].astype(BF16)
            ap_t[here, :] = ap
            pre = dot(fac_a[0, k], ap, 0, 0)
            cdf = 0.5 * (1.0 + lax.erf(pre * inv_sqrt_two))
            h_t[here, :] = (pre * cdf).astype(BF16)
            slope = cdf + pre * jnp.exp(-0.5 * pre * pre) * inv_sqrt_two_pi
            slope_t[here, :] = slope
            gh = dot(fac_b[0, k], gc_t[at_block(block, bs), :].astype(BF16), 1, 0)
            rows_b[u] = rounded(dot(fac_a[0, k], (gh * slope).astype(BF16), 1, 0))
            scatter_rows(perm, block * bs, rows_b.at[u], ga_t, bs)

        each_block(one)

    @pl.when(phase == 2)
    def _():
        def one(k, u):
            cols = at_block(c * STEP + k, bs)
            value = dot(ga_t[cols, :].astype(BF16), fac_a[0, k], 0, 1)
            gn[:, cols] = value
            acc[...] += value * gamma[:, cols] * zed_block(x, scale, cols)

        each_block(one)

    @pl.when(jnp.logical_and(phase == 2, c == pl.num_programs(1) - 1))
    def _():
        mean = jnp.sum(acc[...], axis=1, keepdims=True) / x.shape[1]
        acc[...] = jnp.broadcast_to(mean, acc.shape)

    @pl.when(phase == 3)
    def _():
        def one(k, u):
            here = at_block(k, bs)
            cols = at_block(c * STEP + k, bs)
            z = zed_block(x, scale, cols)
            grad_x[:, here] = gradient(seeded_block(cot, live, here), gn[:, cols], gamma[:, cols], z, scale, acc)

        each_block(one, unroll=4)


def forward_second(perm, h_t, fac, cp_t, c_t, rows):
    phase, c = pl.program_id(0), pl.program_id(1)
    bs = fac.shape[2]

    @pl.when(phase == 0)
    def _():
        each_block(
            lambda k, u: c_t.__setitem__(
                (at_block(c * STEP + k, bs), slice(None)), rounded(dot(fac[0, k], h_t[at_block(k, bs), :], 0, 0))
            )
        )

    @pl.when(phase == 1)
    def _():
        def one(k, u):
            gather_rows(perm, (c * STEP + k) * bs, c_t, rows.at[u], bs)
            cp_t[at_block(k, bs), :] = rows[u].astype(BF16)

        each_block(one)


def each_split(flags, own, body):
    for k in range(STEP // 2):
        group, within = divmod(k, own)
        base = group * 2 * own + within
        body(0, k, base + flags[0] * own)
        body(1, k, base + (1 - flags[0]) * own)


def chosen_gy(flags, cot, live, moved, cols):
    return jnp.where(flags[1] == 1, seeded_block(cot, live, cols), moved[:, cols])


def grad_three(own, flags, cot, live, moved, cp_t, keep, send):
    bs = live.shape[1]
    outs = (keep, send)

    def one(goes, k, block):
        at = at_block(block, bs)
        outs[goes][k] = dot(cp_t[at, :], chosen_gy(flags, cot, live, moved, at), 1, 0).astype(BF16)

    each_split(flags, own, one)


def back_three(perm, flags, cot, live, moved, fac, gc_out, gc_t, rows):
    c = pl.program_id(0)
    bs = fac.shape[2]

    def one(k, u):
        rows[u] = rounded(dot(fac[0, k], chosen_gy(flags, cot, live, moved, at_block(k, bs)), 1, 1))
        scatter_rows(perm, (c * STEP + k) * bs, rows.at[u], gc_t, bs)

    each_block(one)

    @pl.when(c == pl.num_programs(0) - 1)
    def _():
        gc_out[...] = gc_t[...].astype(BF16)


def back_two_one(own, perm, flags, gc_t, h_t, ap_t, slope_t, fac_two, fac_one, keep, send, ga_out, ga_t, gpre, rows):
    c = pl.program_id(0)
    bs = fac_two.shape[2]
    outs = (keep, send)

    def one(k, u):
        here = at_block(k, bs)
        gh = dot(fac_two[0, k], gc_t[here, :], 1, 0)
        gpre[here, :] = (gh * slope_t[here, :]).astype(BF16)
        rows[u] = rounded(dot(fac_one[0, k], gpre[here, :], 1, 0))
        scatter_rows(perm, (c * STEP + k) * bs, rows.at[u], ga_t, bs)

    each_block(one)

    def grads(goes, k, block):
        at = at_block(block, bs)
        outs[goes][0, k] = dot(h_t[at, :], gc_t[at, :], 1, 1).astype(BF16)
        outs[goes][1, k] = dot(ap_t[at, :], gpre[at, :], 1, 1).astype(BF16)

    each_split(flags, own, grads)

    @pl.when(c == pl.num_programs(0) - 1)
    def _():
        ga_out[...] = ga_t[...].astype(BF16)


def back_zero(own, flags, ga_t, x, scale, gamma, fac, keep, send, gn, inner, acc):
    c = pl.program_id(0)
    bs = fac.shape[2]
    outs = (keep, send)

    @pl.when(c == 0)
    def _():
        acc[...] = jnp.zeros(acc.shape, F32)

    def one(goes, k, block):
        at = at_block(block, bs)
        z = zed_block(x, scale, at)
        zg = z * gamma[:, at]
        outs[goes][k, pl.ds(0, bs), :] = dot(ga_t[at, :], zg.astype(BF16), 1, 0).astype(BF16)
        value = dot(ga_t[at, :], fac[0, block], 0, 1)
        gn[:, at] = value
        total = jnp.sum(value * z, axis=0, keepdims=True)
        outs[goes][k, pl.ds(bs, EXTRA), :] = jnp.broadcast_to(total, (EXTRA, bs)).astype(BF16)
        acc[...] += value * zg

    each_split(flags, own, one)

    @pl.when(c == pl.num_programs(0) - 1)
    def _():
        mean = jnp.sum(acc[...], axis=1, keepdims=True) / (x.shape[1] * pl.num_programs(0))
        inner[...] = jnp.broadcast_to(mean, inner.shape)


def back_last(flags, gn, cot, live, moved, x, scale, gamma, inner, grad_x):
    bs = live.shape[1]

    def one(k, u):
        cols = at_block(k, bs)
        z = zed_block(x, scale, cols)
        gy = chosen_gy(flags, cot, live, moved, cols)
        grad_x[:, cols] = gradient(gy, gn[:, cols], gamma[:, cols], z, scale, inner)

    each_block(one, unroll=4)


class Halving:
    def __init__(self, keep, send, order, own, me, replicas):
        self.keep, self.send, self.order = keep, send, list(order)
        self.left = list(range(replicas.bit_length() - 1))[::-1]
        self.left.remove(self.order[0])
        self.own, self.me, self.replicas = own, me, replicas

    def go(self):
        bit = self.order.pop(0)
        self.came = lax.ppermute(self.send, "dp", [(i, i ^ (1 << bit)) for i in range(self.replicas)])
        return self

    def add(self):
        if not self.order:
            self.keep = self.keep.astype(F32) + self.came.astype(F32)
            return self
        bit = self.order[0]
        place = self.left.index(bit)
        shape = (2**place, 2, 2 ** (len(self.left) - 1 - place) * self.own) + self.keep.shape[1:]
        mine = (self.me >> bit) & 1
        keep, came = self.keep.reshape(shape), self.came.reshape(shape)

        def part(which):
            a = lax.dynamic_index_in_dim(keep, which, 1, keepdims=False)
            b = lax.dynamic_index_in_dim(came, which, 1, keepdims=False)
            total = (a.astype(F32) + b.astype(F32)).astype(self.keep.dtype)
            return total.reshape((shape[0] * shape[2],) + shape[3:])

        self.left.remove(bit)
        self.send, self.keep = part(1 - mine), part(mine)
        return self

    def finish(self):
        while self.order:
            self.go().add()
        return self.keep / self.replicas


def on_device(replicas, sections, activations, cotangent, token_ids, gains, factors, monarch_perm):
    x = activations[0]
    gamma = gains
    fac = factors[0]
    perm = monarch_perm[0]
    tokens, width = x.shape
    blocks, bs = fac.shape[1], fac.shape[2]
    own = blocks // replicas
    steps = blocks // STEP
    here = lax.axis_index("section")
    me = lax.axis_index("dp")
    live = jnp.broadcast_to((token_ids != 0).astype(F32)[:, None], (tokens, bs))
    flags = jnp.stack([me & 1, (here == sections - 1).astype(jnp.int32)])
    bits = list(range(replicas.bit_length() - 1))
    other = bits[:1] + bits[2:3] + bits[1:2] + bits[3:]

    tok = whole(tokens, width)
    sca = whole(tokens, bs)
    gam = whole(1, width)
    chunk = (STEP * bs, tokens)
    wide = (tokens, STEP * bs)
    fblock = (1, STEP, bs, bs)
    f_at = lambda which: pl.BlockSpec(fblock, lambda c, *_: (which, c, 0, 0))
    c_at = pl.BlockSpec(chunk, lambda c, *_: (c, 0))
    w_at = pl.BlockSpec(wide, lambda c, *_: (0, c))
    g_at = pl.BlockSpec((1, STEP * bs), lambda c, *_: (0, c))
    feat = lambda dt: jax.ShapeDtypeStruct((width, tokens), dt)
    row = lambda dt: jax.ShapeDtypeStruct((tokens, width), dt)
    small = jax.ShapeDtypeStruct((tokens, bs), F32)
    half = lambda n=0, lead=(): jax.ShapeDtypeStruct(lead + (blocks // 2, bs + n, bs), BF16)
    half_at = pl.BlockSpec((STEP // 2, bs, bs), lambda c, *_: (c, 0, 0))
    more_at = pl.BlockSpec((STEP // 2, bs + EXTRA, bs), lambda c, *_: (c, 0, 0))
    two_at = pl.BlockSpec((2, STEP // 2, bs, bs), lambda c, *_: (0, c, 0, 0))
    big = pltpu.VMEM((width, tokens), F32)
    rows = pltpu.VMEM((UNROLL, bs, tokens), F32)
    last = steps - 1

    def phased(*picks):
        def at(ph, c):
            out = c if picks[-1] is None else picks[-1]
            for i in range(len(picks) - 2, -1, -1):
                out = jnp.where(ph == i, c if picks[i] is None else picks[i], out)
            return out

        return at

    pick = lambda values: lambda ph: jnp.where(ph == 0, values[0], jnp.where(ph == 1, values[1], values[2]))
    a_which, a_at = pick((0, 1, 0)), phased(None, None, None, last)
    b_which, b_at = pick((3, 2, 2)), phased(None, None, last, last)
    cot_at, out_at, mid_at = phased(None, last, last, None), phased(0, 0, 0, None), phased(0, None, last, last)
    mid = pl.BlockSpec(chunk, lambda ph, c, *_: (mid_at(ph, c), 0))
    ap_t, h_t, slope_t, scale, grad_x = call(
        first_pass,
        "first_pass",
        (4, steps),
        [
            tok,
            pl.BlockSpec(wide, lambda ph, c, *_: (0, cot_at(ph, c))),
            sca,
            gam,
            pl.BlockSpec(fblock, lambda ph, c, *_: (a_which(ph), a_at(ph, c), 0, 0)),
            pl.BlockSpec(fblock, lambda ph, c, *_: (b_which(ph), b_at(ph, c), 0, 0)),
        ],
        [mid, mid, mid, sca, pl.BlockSpec(wide, lambda ph, c, *_: (0, out_at(ph, c)))],
        [feat(BF16), feat(BF16), feat(F32), small, row(BF16)],
        [big, big, big, pltpu.VMEM((tokens, width), F32), pltpu.VMEM((tokens, bs), F32), rows, rows],
    )(perm, x, cotangent, live, gamma, fac, fac)
    moved = lax.ppermute(grad_x, "section", [(i, i - 1) for i in range(1, sections)])

    early, rest = phased(None, last), phased(0, None)
    cp_t = call(
        forward_second,
        "forward_second",
        (2, steps),
        [
            pl.BlockSpec(chunk, lambda ph, c, *_: (early(ph, c), 0)),
            pl.BlockSpec(fblock, lambda ph, c, *_: (2, early(ph, c), 0, 0)),
        ],
        pl.BlockSpec(chunk, lambda ph, c, *_: (rest(ph, c), 0)),
        feat(BF16),
        [big, rows],
    )(perm, h_t, fac)

    start = lambda keep, send, order: Halving(keep, send, order, own, me, replicas)
    keep, send = call(
        functools.partial(grad_three, own),
        "grad_three",
        (steps,),
        [w_at, sca, w_at, c_at],
        [half_at, half_at],
        [half(), half()],
    )(flags, cotangent, live, moved, cp_t)
    three = start(keep, send, bits).go()
    gc_t = call(
        back_three,
        "back_three",
        (steps,),
        [w_at, sca, w_at, f_at(3)],
        whole(width, tokens),
        feat(BF16),
        [big, rows],
        prefetch=2,
    )(perm, flags, cotangent, live, moved, fac)
    gc_t, three.keep, three.came = lax.optimization_barrier((gc_t, three.keep, three.came))
    three.add()
    gc_t, three.keep, three.send = lax.optimization_barrier((gc_t, three.keep, three.send))
    three.go()
    keep, send, ga_t = call(
        functools.partial(back_two_one, own),
        "back_two_one",
        (steps,),
        [c_at, c_at, c_at, c_at, f_at(2), f_at(1)],
        [two_at, two_at, whole(width, tokens)],
        [half(0, (2,)), half(0, (2,)), feat(BF16)],
        [big, pltpu.VMEM(chunk, BF16), rows],
        prefetch=2,
    )(perm, flags, gc_t, h_t, ap_t, slope_t, fac, fac)
    came = lax.ppermute(send, "dp", [(i, i ^ 1) for i in range(replicas)])
    keep_zero, send_zero, gn, inner = call(
        functools.partial(back_zero, own),
        "back_zero",
        (steps,),
        [c_at, w_at, sca, g_at, f_at(0)],
        [more_at, more_at, w_at, sca],
        [half(EXTRA), half(EXTRA), row(F32), small],
        [pltpu.VMEM((tokens, bs), F32)],
    )(flags, ga_t, x, scale, gamma, fac)
    zero = start(keep_zero, send_zero, bits).go()
    gn, keep, came, three.keep, three.came = lax.optimization_barrier((gn, keep, came, three.keep, three.came))
    two, one = start(keep[0], None, other), start(keep[1], None, bits)
    for each, i in ((two, 0), (one, 1)):
        each.order.pop(0)
        each.came = came[i]
        each.add()
    three.add()
    gn, two.keep, two.send, one.keep, one.send, three.keep, three.send = lax.optimization_barrier(
        (gn, two.keep, two.send, one.keep, one.send, three.keep, three.send)
    )
    three.go()
    one.go()
    two.go()
    out_grad = call(
        back_last,
        "back_last",
        (steps,),
        [w_at, w_at, sca, w_at, w_at, sca, g_at, sca],
        w_at,
        row(BF16),
    )(flags, gn, cotangent, live, moved, x, scale, gamma, inner)
    zero.add()
    for each in (three, one, two):
        each.add()
    total = [each.finish() for each in (zero, one, two, three)]
    grad_gamma = total[0][:, bs, :].reshape(1, own * bs)
    total[0] = jnp.swapaxes(total[0][:, :bs, :], 1, 2)
    return (out_grad[None], jnp.stack(total)[None], grad_gamma)


def solution(mesh):
    replicas, sections = mesh.shape["dp"], mesh.shape["section"]
    in_specs = (
        P("section", "dp", None),
        P("dp", None),
        P("dp"),
        P("section", None),
        P("section", None, None, None, None),
        P("section", None),
    )
    out_specs = (P("section", "dp", None), P("section", None, "dp", None, None), P("section", "dp"))
    return jax.shard_map(
        functools.partial(on_device, replicas, sections),
        mesh=mesh,
        in_specs=in_specs,
        out_specs=out_specs,
        check_vma=False,
    )
```

```python
import functools

import jax
import jax.numpy as jnp
from jax import lax
from jax.experimental import pallas as pl
from jax.experimental.pallas import tpu as pltpu
from jax.sharding import PartitionSpec as P

F32 = jnp.float32
BF16 = jnp.bfloat16
inv_sqrt_two = 0.7071067811865476
inv_sqrt_two_pi = 0.3989422804014327
STEP = 16
UNROLL = 8
EXTRA = 16


def dot(a, b, ca, cb):
    return lax.dot_general(a, b, (((ca,), (cb,)), ((), ())), preferred_element_type=F32)


def whole(*shape):
    return pl.BlockSpec(shape, lambda *_: (0,) * len(shape))


def call(body, name, grid, in_specs, out_specs, out_shape, scratch=(), prefetch=1, vmem=50):
    return pl.pallas_call(
        body,
        name=name,
        out_shape=out_shape,
        grid_spec=pltpu.PrefetchScalarGridSpec(
            num_scalar_prefetch=prefetch,
            grid=grid,
            in_specs=in_specs,
            out_specs=out_specs,
            scratch_shapes=scratch,
        ),
        compiler_params=pltpu.CompilerParams(vmem_limit_bytes=vmem << 20),
    )


def each_block(body, count=STEP, unroll=UNROLL):
    def some(i, carry):
        for u in range(unroll):
            body(i * unroll + u, u)
        return carry

    lax.fori_loop(0, count // unroll, some, 0)


def at_block(k, bs):
    return pl.ds(pl.multiple_of(k * bs, bs), bs)


def rounded(v):
    return v.astype(BF16).astype(F32)


def zed_block(x, scale, cols):
    return x[:, cols].astype(F32) * scale[...]


def gather_rows(perm, base, source, target, count):
    for i in range(count):
        target[pl.ds(i, 1), :] = source[pl.ds(perm[base + i], 1), :]


def scatter_rows(perm, base, source, target, count):
    for i in range(count):
        target[pl.ds(perm[base + i], 1), :] = source[pl.ds(i, 1), :]


def seeded_block(cot, live, cols):
    return (cot[:, cols].astype(F32) * live[...]).astype(BF16)


def gradient(gy, gn, gamma, z, scale, inner):
    return (gy.astype(F32) + scale[...] * (gn * gamma - z * inner[...])).astype(BF16)


def first_pass(perm, x, cot, live, gamma, fac_a, fac_b, ap_t, h_t, slope_t, scale, grad_x, a_t, gc_t, ga_t, gn, acc, rows, rows_b):
    phase, c = pl.program_id(0), pl.program_id(1)
    bs = fac_a.shape[2]
    blocks = x.shape[1] // bs

    @pl.when(jnp.logical_and(phase == 0, c == 0))
    def _():
        def add(k, total):
            xk = x[:, at_block(k, bs)].astype(F32)
            return total + xk * xk

        total = lax.fori_loop(0, blocks, add, jnp.zeros((x.shape[0], bs), F32), unroll=8)
        mean = jnp.sum(total, axis=1, keepdims=True) / x.shape[1]
        scale[...] = jnp.broadcast_to(lax.rsqrt(mean + 1e-06), scale.shape)
        acc[...] = jnp.zeros(acc.shape, F32)

    @pl.when(phase == 0)
    def _():
        def one(k, u):
            block = c * STEP + k
            cols = at_block(block, bs)
            n = (zed_block(x, scale, cols) * gamma[:, cols]).astype(BF16)
            a_t[cols, :] = rounded(dot(fac_a[0, k], n, 0, 1))
            rows[u] = rounded(dot(fac_b[0, k], seeded_block(cot, live, at_block(k, bs)), 1, 1))
            scatter_rows(perm, block * bs, rows.at[u], gc_t, bs)

        each_block(one)

    @pl.when(phase == 1)
    def _():
        def one(k, u):
            block = c * STEP + k
            here = at_block(k, bs)
            gather_rows(perm, block * bs, a_t, rows.at[u], bs)
            ap = rows[u].astype(BF16)
            ap_t[here, :] = ap
            pre = dot(fac_a[0, k], ap, 0, 0)
            cdf = 0.5 * (1.0 + lax.erf(pre * inv_sqrt_two))
            h_t[here, :] = (pre * cdf).astype(BF16)
            slope = cdf + pre * jnp.exp(-0.5 * pre * pre) * inv_sqrt_two_pi
            slope_t[here, :] = slope
            gh = dot(fac_b[0, k], gc_t[at_block(block, bs), :].astype(BF16), 1, 0)
            rows_b[u] = rounded(dot(fac_a[0, k], (gh * slope).astype(BF16), 1, 0))
            scatter_rows(perm, block * bs, rows_b.at[u], ga_t, bs)

        each_block(one)

    @pl.when(phase == 2)
    def _():
        def one(k, u):
            cols = at_block(c * STEP + k, bs)
            value = dot(ga_t[cols, :].astype(BF16), fac_a[0, k], 0, 1)
            gn[:, cols] = value
            acc[...] += value * gamma[:, cols] * zed_block(x, scale, cols)

        each_block(one)

    @pl.when(jnp.logical_and(phase == 2, c == pl.num_programs(1) - 1))
    def _():
        mean = jnp.sum(acc[...], axis=1, keepdims=True) / x.shape[1]
        acc[...] = jnp.broadcast_to(mean, acc.shape)

    @pl.when(phase == 3)
    def _():
        def one(k, u):
            here = at_block(k, bs)
            cols = at_block(c * STEP + k, bs)
            z = zed_block(x, scale, cols)
            grad_x[:, here] = gradient(seeded_block(cot, live, here), gn[:, cols], gamma[:, cols], z, scale, acc)

        each_block(one, unroll=4)


def forward_second(perm, h_t, fac, cp_t, c_t, rows):
    phase, c = pl.program_id(0), pl.program_id(1)
    bs = fac.shape[2]

    @pl.when(phase == 0)
    def _():
        each_block(
            lambda k, u: c_t.__setitem__(
                (at_block(c * STEP + k, bs), slice(None)), rounded(dot(fac[0, k], h_t[at_block(k, bs), :], 0, 0))
            )
        )

    @pl.when(phase == 1)
    def _():
        def one(k, u):
            gather_rows(perm, (c * STEP + k) * bs, c_t, rows.at[u], bs)
            cp_t[at_block(k, bs), :] = rows[u].astype(BF16)

        each_block(one)


def each_split(flags, own, body):
    for k in range(STEP // 2):
        group, within = divmod(k, own)
        base = group * 2 * own + within
        body(0, k, base + flags[0] * own)
        body(1, k, base + (1 - flags[0]) * own)


def chosen_gy(flags, cot, live, moved, cols):
    return jnp.where(flags[1] == 1, seeded_block(cot, live, cols), moved[:, cols])


def grad_three(own, flags, cot, live, moved, cp_t, keep, send):
    bs = live.shape[1]
    outs = (keep, send)

    def one(goes, k, block):
        at = at_block(block, bs)
        outs[goes][k] = dot(cp_t[at, :], chosen_gy(flags, cot, live, moved, at), 1, 0).astype(BF16)

    each_split(flags, own, one)


def back_three(perm, flags, cot, live, moved, fac, gc_out, gc_t, rows):
    c = pl.program_id(0)
    bs = fac.shape[2]

    def one(k, u):
        rows[u] = rounded(dot(fac[0, k], chosen_gy(flags, cot, live, moved, at_block(k, bs)), 1, 1))
        scatter_rows(perm, (c * STEP + k) * bs, rows.at[u], gc_t, bs)

    each_block(one)

    @pl.when(c == pl.num_programs(0) - 1)
    def _():
        gc_out[...] = gc_t[...].astype(BF16)


def back_two_one(
    own, perm, flags, gc_t, h_t, ap_t, slope_t, fac_two, fac_one, keep_two, send_two, keep_one, send_one, ga_out, ga_t, gpre, rows
):
    c = pl.program_id(0)
    bs = fac_two.shape[2]
    twos, ones = (keep_two, send_two), (keep_one, send_one)

    def one(k, u):
        here = at_block(k, bs)
        gh = dot(fac_two[0, k], gc_t[here, :], 1, 0)
        gpre[here, :] = (gh * slope_t[here, :]).astype(BF16)
        rows[u] = rounded(dot(fac_one[0, k], gpre[here, :], 1, 0))
        scatter_rows(perm, (c * STEP + k) * bs, rows.at[u], ga_t, bs)

    each_block(one)

    def grads(goes, k, block):
        at = at_block(block, bs)
        twos[goes][k] = dot(h_t[at, :], gc_t[at, :], 1, 1).astype(BF16)
        ones[goes][k] = dot(ap_t[at, :], gpre[at, :], 1, 1).astype(BF16)

    each_split(flags, own, grads)

    @pl.when(c == pl.num_programs(0) - 1)
    def _():
        ga_out[...] = ga_t[...].astype(BF16)


def back_zero(own, flags, ga_t, x, scale, gamma, fac, keep, send, gn, inner, acc):
    c = pl.program_id(0)
    bs = fac.shape[2]
    outs = (keep, send)

    @pl.when(c == 0)
    def _():
        acc[...] = jnp.zeros(acc.shape, F32)

    def one(goes, k, block):
        at = at_block(block, bs)
        z = zed_block(x, scale, at)
        zg = z * gamma[:, at]
        outs[goes][k, pl.ds(0, bs), :] = dot(zg.astype(BF16), ga_t[at, :], 0, 1).astype(BF16)
        value = dot(ga_t[at, :], fac[0, block], 0, 1)
        gn[:, at] = value
        total = jnp.sum(value * z, axis=0, keepdims=True)
        outs[goes][k, pl.ds(bs, EXTRA), :] = jnp.broadcast_to(total, (EXTRA, bs)).astype(BF16)
        acc[...] += value * zg

    each_split(flags, own, one)

    @pl.when(c == pl.num_programs(0) - 1)
    def _():
        mean = jnp.sum(acc[...], axis=1, keepdims=True) / (x.shape[1] * pl.num_programs(0))
        inner[...] = jnp.broadcast_to(mean, inner.shape)


def back_last(flags, gn, cot, live, moved, x, scale, gamma, inner, grad_x):
    bs = live.shape[1]

    def one(k, u):
        cols = at_block(k, bs)
        z = zed_block(x, scale, cols)
        gy = chosen_gy(flags, cot, live, moved, cols)
        grad_x[:, cols] = gradient(gy, gn[:, cols], gamma[:, cols], z, scale, inner)

    each_block(one, unroll=4)


class Halving:
    def __init__(self, keep, send, order, own, me, replicas):
        self.keep, self.send, self.order = keep, send, list(order)
        self.left = list(range(replicas.bit_length() - 1))[::-1]
        self.left.remove(self.order[0])
        self.own, self.me, self.replicas = own, me, replicas
        self.came = None

    def go(self):
        bit = self.order.pop(0)
        self.came = lax.ppermute(self.send, "dp", [(i, i ^ (1 << bit)) for i in range(self.replicas)])
        return self

    def add(self):
        if not self.order:
            self.keep, self.send, self.came = self.keep.astype(F32) + self.came.astype(F32), None, None
            return self
        bit = self.order[0]
        place = self.left.index(bit)
        shape = (2**place, 2, 2 ** (len(self.left) - 1 - place) * self.own) + self.keep.shape[1:]
        mine = (self.me >> bit) & 1
        keep, came = self.keep.reshape(shape), self.came.reshape(shape)

        def part(which):
            a = lax.dynamic_index_in_dim(keep, which, 1, keepdims=False)
            b = lax.dynamic_index_in_dim(came, which, 1, keepdims=False)
            total = (a.astype(F32) + b.astype(F32)).astype(self.keep.dtype)
            return total.reshape((shape[0] * shape[2],) + shape[3:])

        self.left.remove(bit)
        self.send, self.keep = part(1 - mine), part(mine)
        self.came = None
        return self

    def finish(self):
        if self.came is not None:
            self.add()
        while self.order:
            self.go().add()
        return self.keep / self.replicas


def met(*halvings, then):
    state = [(h.keep, h.send if h.came is None else h.came) for h in halvings]
    state, then = lax.optimization_barrier((state, then))
    for h, (keep, rest) in zip(halvings, state):
        h.keep = keep
        if h.came is None:
            h.send = rest
        else:
            h.came = rest
    return then


def on_device(replicas, sections, activations, cotangent, token_ids, gains, factors, monarch_perm):
    x = activations[0]
    gamma = gains
    fac = factors[0]
    perm = monarch_perm[0]
    tokens, width = x.shape
    blocks, bs = fac.shape[1], fac.shape[2]
    own = blocks // replicas
    steps = blocks // STEP
    here = lax.axis_index("section")
    me = lax.axis_index("dp")
    live = jnp.broadcast_to((token_ids != 0).astype(F32)[:, None], (tokens, bs))
    flags = jnp.stack([me & 1, (here == sections - 1).astype(jnp.int32)])
    bits = list(range(replicas.bit_length() - 1))
    other = bits[:1] + bits[2:3] + bits[1:2] + bits[3:]

    tok = whole(tokens, width)
    sca = whole(tokens, bs)
    gam = whole(1, width)
    chunk = (STEP * bs, tokens)
    wide = (tokens, STEP * bs)
    fblock = (1, STEP, bs, bs)
    f_at = lambda which: pl.BlockSpec(fblock, lambda c, *_: (which, c, 0, 0))
    c_at = pl.BlockSpec(chunk, lambda c, *_: (c, 0))
    w_at = pl.BlockSpec(wide, lambda c, *_: (0, c))
    g_at = pl.BlockSpec((1, STEP * bs), lambda c, *_: (0, c))
    feat = lambda dt: jax.ShapeDtypeStruct((width, tokens), dt)
    row = lambda dt: jax.ShapeDtypeStruct((tokens, width), dt)
    small = jax.ShapeDtypeStruct((tokens, bs), F32)
    half = lambda n=0, lead=(): jax.ShapeDtypeStruct(lead + (blocks // 2, bs + n, bs), BF16)
    half_at = pl.BlockSpec((STEP // 2, bs, bs), lambda c, *_: (c, 0, 0))
    more_at = pl.BlockSpec((STEP // 2, bs + EXTRA, bs), lambda c, *_: (c, 0, 0))
    two_at = pl.BlockSpec((2, STEP // 2, bs, bs), lambda c, *_: (0, c, 0, 0))
    big = pltpu.VMEM((width, tokens), F32)
    rows = pltpu.VMEM((UNROLL, bs, tokens), F32)
    last = steps - 1

    def phased(*picks):
        def at(ph, c):
            out = c if picks[-1] is None else picks[-1]
            for i in range(len(picks) - 2, -1, -1):
                out = jnp.where(ph == i, c if picks[i] is None else picks[i], out)
            return out

        return at

    pick = lambda values: lambda ph: jnp.where(ph == 0, values[0], jnp.where(ph == 1, values[1], values[2]))
    a_which, a_at = pick((0, 1, 0)), phased(None, None, None, last)
    b_which, b_at = pick((3, 2, 2)), phased(None, None, last, last)
    cot_at, out_at, mid_at = phased(None, last, last, None), phased(0, 0, 0, None), phased(0, None, last, last)
    mid = pl.BlockSpec(chunk, lambda ph, c, *_: (mid_at(ph, c), 0))
    ap_t, h_t, slope_t, scale, grad_x = call(
        first_pass,
        "first_pass",
        (4, steps),
        [
            tok,
            pl.BlockSpec(wide, lambda ph, c, *_: (0, cot_at(ph, c))),
            sca,
            gam,
            pl.BlockSpec(fblock, lambda ph, c, *_: (a_which(ph), a_at(ph, c), 0, 0)),
            pl.BlockSpec(fblock, lambda ph, c, *_: (b_which(ph), b_at(ph, c), 0, 0)),
        ],
        [mid, mid, mid, sca, pl.BlockSpec(wide, lambda ph, c, *_: (0, out_at(ph, c)))],
        [feat(BF16), feat(BF16), feat(F32), small, row(BF16)],
        [big, big, big, pltpu.VMEM((tokens, width), F32), pltpu.VMEM((tokens, bs), F32), rows, rows],
        vmem=50,
    )(perm, x, cotangent, live, gamma, fac, fac)
    moved = lax.ppermute(grad_x, "section", [(i, i - 1) for i in range(1, sections)])

    early, rest = phased(None, last), phased(0, None)
    cp_t = call(
        forward_second,
        "forward_second",
        (2, steps),
        [
            pl.BlockSpec(chunk, lambda ph, c, *_: (early(ph, c), 0)),
            pl.BlockSpec(fblock, lambda ph, c, *_: (2, early(ph, c), 0, 0)),
        ],
        pl.BlockSpec(chunk, lambda ph, c, *_: (rest(ph, c), 0)),
        feat(BF16),
        [big, rows],
    )(perm, h_t, fac)

    start = lambda keep, send, order: Halving(keep, send, order, own, me, replicas)
    keep, send = call(
        functools.partial(grad_three, own),
        "grad_three",
        (steps,),
        [w_at, sca, w_at, c_at],
        [half_at, half_at],
        [half(), half()],
    )(flags, cotangent, live, moved, cp_t)
    three = start(keep, send, bits).go()
    gc_t = call(
        back_three,
        "back_three",
        (steps,),
        [w_at, sca, w_at, f_at(3)],
        whole(width, tokens),
        feat(BF16),
        [big, rows],
        prefetch=2,
    )(perm, flags, cotangent, live, moved, fac)
    (gc_t,) = met(three, then=[gc_t])
    three.add()
    (gc_t,) = met(three, then=[gc_t])
    three.go()
    keep_two, send_two, keep_one, send_one, ga_t = call(
        functools.partial(back_two_one, own),
        "back_two_one",
        (steps,),
        [c_at, c_at, c_at, c_at, f_at(2), f_at(1)],
        [half_at] * 4 + [whole(width, tokens)],
        [half()] * 4 + [feat(BF16)],
        [big, pltpu.VMEM(chunk, BF16), rows],
        prefetch=2,
    )(perm, flags, gc_t, h_t, ap_t, slope_t, fac, fac)
    two, one = start(keep_two, send_two, other), start(keep_one, send_one, bits)
    ga_t, one.keep, one.send, two.keep, two.send = met(three, then=[ga_t, one.keep, one.send, two.keep, two.send])
    three.add()
    (ga_t,) = met(three, then=[ga_t])
    one.go()
    two.go()
    three.go()
    keep_zero, send_zero, gn, inner = call(
        functools.partial(back_zero, own),
        "back_zero",
        (steps,),
        [c_at, w_at, sca, g_at, f_at(0)],
        [more_at, more_at, w_at, sca],
        [half(EXTRA), half(EXTRA), row(F32), small],
        [pltpu.VMEM((tokens, bs), F32)],
    )(flags, ga_t, x, scale, gamma, fac)
    zero = start(keep_zero, send_zero, bits)
    gn, zero.keep, zero.send = met(one, two, three, then=[gn, zero.keep, zero.send])
    zero.go()
    for each in (one, two, three):
        each.add()
    (gn,) = met(one, two, three, then=[gn])
    for each in (one, two, three):
        each.go()
    out_grad = call(
        back_last,
        "back_last",
        (steps,),
        [w_at, w_at, sca, w_at, w_at, sca, g_at, sca],
        w_at,
        row(BF16),
    )(flags, gn, cotangent, live, moved, x, scale, gamma, inner)
    (out_grad,) = met(zero, then=[out_grad])
    zero.add()
    (out_grad,) = met(zero, one, two, three, then=[out_grad])
    zero.go()
    for each in (one, two, three):
        each.add()
    total = [each.finish() for each in (zero, one, two, three)]
    grad_gamma = total[0][:, bs, :].reshape(1, own * bs)
    total[0] = total[0][:, :bs, :]
    return (out_grad[None], jnp.stack(total)[None], grad_gamma)


def solution(mesh):
    replicas, sections = mesh.shape["dp"], mesh.shape["section"]
    in_specs = (
        P("section", "dp", None),
        P("dp", None),
        P("dp"),
        P("section", None),
        P("section", None, None, None, None),
        P("section", None),
    )
    out_specs = (P("section", "dp", None), P("section", None, "dp", None, None), P("section", "dp"))
    return jax.shard_map(
        functools.partial(on_device, replicas, sections),
        mesh=mesh,
        in_specs=in_specs,
        out_specs=out_specs,
        check_vma=False,
    )
```

```python
import functools

import jax
import jax.numpy as jnp
from jax import lax
from jax.experimental import pallas as pl
from jax.experimental.pallas import tpu as pltpu
from jax.sharding import PartitionSpec as P

F32 = jnp.float32
BF16 = jnp.bfloat16
inv_sqrt_two = 0.7071067811865476
inv_sqrt_two_pi = 0.3989422804014327
STEP = 16
UNROLL = 8
EXTRA = 16


def dot(a, b, ca, cb):
    return lax.dot_general(a, b, (((ca,), (cb,)), ((), ())), preferred_element_type=F32)


def whole(*shape):
    return pl.BlockSpec(shape, lambda *_: (0,) * len(shape))


def call(body, name, grid, in_specs, out_specs, out_shape, scratch=(), prefetch=1, vmem=50, aliases=None):
    return pl.pallas_call(
        body,
        name=name,
        input_output_aliases=aliases or {},
        out_shape=out_shape,
        grid_spec=pltpu.PrefetchScalarGridSpec(
            num_scalar_prefetch=prefetch,
            grid=grid,
            in_specs=in_specs,
            out_specs=out_specs,
            scratch_shapes=scratch,
        ),
        compiler_params=pltpu.CompilerParams(vmem_limit_bytes=vmem << 20),
    )


def each_block(body, count=STEP, unroll=UNROLL):
    def some(i, carry):
        for u in range(unroll):
            body(i * unroll + u, u)
        return carry

    lax.fori_loop(0, count // unroll, some, 0)


def at_block(k, bs):
    return pl.ds(pl.multiple_of(k * bs, bs), bs)


def rounded(v):
    return v.astype(BF16).astype(F32)


def zed_block(x, scale, cols):
    return x[:, cols].astype(F32) * scale[...]


def gather_rows(perm, base, source, target, count):
    for i in range(count):
        target[pl.ds(i, 1), :] = source[pl.ds(perm[base + i], 1), :]


def scatter_rows(perm, base, source, target, count):
    for i in range(count):
        target[pl.ds(perm[base + i], 1), :] = source[pl.ds(i, 1), :]


def scattered(make, perm, first, target, even, odd, bs):
    def move(k, source):
        scatter_rows(perm, (first + k) * bs, source, target, bs)

    even[...] = make(0)

    def pair(i, carry):
        k = 2 * i
        odd[...] = make(k + 1)
        move(k, even)
        even[...] = make(k + 2)
        move(k + 1, odd)
        return carry

    lax.fori_loop(0, STEP // 2 - 1, pair, 0)
    odd[...] = make(STEP - 1)
    move(STEP - 2, even)
    move(STEP - 1, odd)


def gathered_scattered(make, perm, first, source, target, even_in, odd_in, even_out, odd_out, bs):
    def fetch(k, into):
        gather_rows(perm, (first + k) * bs, source, into, bs)

    def move(k, out):
        scatter_rows(perm, (first + k) * bs, out, target, bs)

    fetch(0, even_in)
    fetch(1, odd_in)
    even_out[...] = make(0, even_in)

    def pair(i, carry):
        k = 2 * i
        odd_out[...] = make(k + 1, odd_in)
        fetch(k + 2, even_in)
        move(k, even_out)
        even_out[...] = make(k + 2, even_in)
        fetch(k + 3, odd_in)
        move(k + 1, odd_out)
        return carry

    lax.fori_loop(0, STEP // 2 - 1, pair, 0)
    odd_out[...] = make(STEP - 1, odd_in)
    move(STEP - 2, even_out)
    move(STEP - 1, odd_out)


def put_split(stage, flags, own, k, value):
    device = lax.div(k, own)
    goes = lax.bitwise_xor(lax.bitwise_and(device, 1), flags[0])
    stage[goes, lax.div(device, 2) * own + lax.rem(k, own)] = value.astype(BF16)


def seeded_block(cot, live, cols):
    return (cot[:, cols].astype(F32) * live[...]).astype(BF16)


def gradient(gy, gn, gamma, z, scale, inner):
    return (gy.astype(F32) + scale[...] * (gn * gamma - z * inner[...])).astype(BF16)


def first_pass(
    perm, x, cot, live, gamma, fac_a, fac_b, ap_t, h_t, slope_t, scale, grad_a, grad_b, a_t, gc_t, ga_t, gn, acc, r0, r1, r2, r3
):
    phase, c = pl.program_id(0), pl.program_id(1)
    bs = fac_a.shape[2]
    blocks = x.shape[1] // bs

    @pl.when(jnp.logical_and(phase == 0, c == 0))
    def _():
        def add(k, total):
            xk = x[:, at_block(k, bs)].astype(F32)
            return total + xk * xk

        total = lax.fori_loop(0, blocks, add, jnp.zeros((x.shape[0], bs), F32), unroll=8)
        mean = jnp.sum(total, axis=1, keepdims=True) / x.shape[1]
        scale[...] = jnp.broadcast_to(lax.rsqrt(mean + 1e-06), scale.shape)
        acc[...] = jnp.zeros(acc.shape, F32)

    @pl.when(phase == 0)
    def _():
        def make(k):
            cols = at_block(c * STEP + k, bs)
            n = (zed_block(x, scale, cols) * gamma[:, cols]).astype(BF16)
            a_t[cols, :] = rounded(dot(fac_a[0, k], n, 0, 1))
            return rounded(dot(fac_b[0, k], seeded_block(cot, live, at_block(k, bs)), 1, 1))

        scattered(make, perm, c * STEP, gc_t, r0, r1, bs)

    @pl.when(phase == 1)
    def _():
        def make(k, rows):
            here = at_block(k, bs)
            ap = rows[...].astype(BF16)
            ap_t[here, :] = ap
            pre = dot(fac_a[0, k], ap, 0, 0)
            cdf = 0.5 * (1.0 + lax.erf(pre * inv_sqrt_two))
            h_t[here, :] = (pre * cdf).astype(BF16)
            slope = cdf + pre * jnp.exp(-0.5 * pre * pre) * inv_sqrt_two_pi
            slope_t[here, :] = slope
            gh = dot(fac_b[0, k], gc_t[at_block(c * STEP + k, bs), :].astype(BF16), 1, 0)
            return rounded(dot(fac_a[0, k], (gh * slope).astype(BF16), 1, 0))

        gathered_scattered(make, perm, c * STEP, a_t, ga_t, r0, r1, r2, r3, bs)

    @pl.when(phase == 2)
    def _():
        def one(k, u):
            cols = at_block(c * STEP + k, bs)
            value = dot(ga_t[cols, :].astype(BF16), fac_a[0, k], 0, 1)
            gn[:, cols] = value
            acc[...] += value * gamma[:, cols] * zed_block(x, scale, cols)

        each_block(one)

    @pl.when(jnp.logical_and(phase == 2, c == pl.num_programs(1) - 1))
    def _():
        mean = jnp.sum(acc[...], axis=1, keepdims=True) / x.shape[1]
        acc[...] = jnp.broadcast_to(mean, acc.shape)

    def emit(out):
        def one(k, u):
            here = at_block(k, bs)
            cols = at_block(c * STEP + k, bs)
            z = zed_block(x, scale, cols)
            out[:, here] = gradient(seeded_block(cot, live, here), gn[:, cols], gamma[:, cols], z, scale, acc)

        each_block(one, unroll=4)

    last = pl.num_programs(1) - 1
    pl.when(jnp.logical_and(phase == 3, c < last))(lambda: emit(grad_a))
    pl.when(jnp.logical_and(phase == 3, c == last))(lambda: emit(grad_b))


def forward_second(perm, h_t, fac, cp_t, c_t, rows):
    phase, c = pl.program_id(0), pl.program_id(1)
    bs = fac.shape[2]

    @pl.when(phase == 0)
    def _():
        each_block(
            lambda k, u: c_t.__setitem__(
                (at_block(c * STEP + k, bs), slice(None)), rounded(dot(fac[0, k], h_t[at_block(k, bs), :], 0, 0))
            )
        )

    @pl.when(phase == 1)
    def _():
        def one(k, u):
            gather_rows(perm, (c * STEP + k) * bs, c_t, rows.at[u], bs)
            cp_t[at_block(k, bs), :] = rows[u].astype(BF16)

        each_block(one)


def each_split(flags, own, body):
    for k in range(STEP // 2):
        group, within = divmod(k, own)
        base = group * 2 * own + within
        body(0, k, base + flags[0] * own)
        body(1, k, base + (1 - flags[0]) * own)


def back_three(own, skipped, perm, flags, cot, live, moved, cp_t, fac, *refs):
    *given, keep, send, gy_out, gc_t, stage, even, odd = refs
    bs = fac.shape[2]
    if given:
        gc_t[...] = given[3][...]

    def make(k):
        here = at_block(k, bs)
        gy = jnp.where(flags[1] == 1, seeded_block(cot, live, here), moved[:, here])
        gy_out[:, here] = gy
        put_split(stage, flags, own, k, dot(cp_t[here, :], gy, 1, 0))
        return rounded(dot(fac[0, k], gy, 1, 1))

    scattered(make, perm, (pl.program_id(0) + skipped) * STEP, gc_t, even, odd, bs)
    keep[...] = stage[0]
    send[...] = stage[1]


def back_two_one(
    own, perm, flags, gc_t, h_t, ap_t, slope_t, fac_two, fac_one, keep_two, send_two, keep_one, send_one, ga_out, ga_t, twos, ones, even, odd
):
    c = pl.program_id(0)
    bs = fac_two.shape[2]

    def make(k):
        here = at_block(k, bs)
        gc = gc_t[here, :].astype(BF16)
        gh = dot(fac_two[0, k], gc, 1, 0)
        gpre = (gh * slope_t[here, :]).astype(BF16)
        put_split(twos, flags, own, k, dot(h_t[here, :], gc, 1, 1))
        put_split(ones, flags, own, k, dot(ap_t[here, :], gpre, 1, 1))
        return rounded(dot(fac_one[0, k], gpre, 1, 0))

    scattered(make, perm, c * STEP, ga_t, even, odd, bs)
    keep_two[...], send_two[...] = twos[0], twos[1]
    keep_one[...], send_one[...] = ones[0], ones[1]

    @pl.when(c == pl.num_programs(0) - 1)
    def _():
        ga_out[...] = ga_t[...].astype(BF16)


def back_zero(own, flags, ga_t, x, scale, gamma, fac, keep, send, gn, inner, acc):
    c = pl.program_id(0)
    bs = fac.shape[2]
    outs = (keep, send)

    @pl.when(c == 0)
    def _():
        acc[...] = jnp.zeros(acc.shape, F32)

    def one(goes, k, block):
        at = at_block(block, bs)
        z = zed_block(x, scale, at)
        zg = z * gamma[:, at]
        outs[goes][k, pl.ds(0, bs), :] = dot(zg.astype(BF16), ga_t[at, :], 0, 1).astype(BF16)
        value = dot(ga_t[at, :], fac[0, block], 0, 1)
        gn[:, at] = value
        total = jnp.sum(value * z, axis=0, keepdims=True)
        outs[goes][k, pl.ds(bs, EXTRA), :] = jnp.broadcast_to(total, (EXTRA, bs)).astype(BF16)
        acc[...] += value * zg

    each_split(flags, own, one)

    @pl.when(c == pl.num_programs(0) - 1)
    def _():
        mean = jnp.sum(acc[...], axis=1, keepdims=True) / (x.shape[1] * pl.num_programs(0))
        inner[...] = jnp.broadcast_to(mean, inner.shape)


def back_last(gy, gn, x, scale, gamma, inner, grad_x):
    bs = scale.shape[1]

    def one(k, u):
        cols = at_block(k, bs)
        z = zed_block(x, scale, cols)
        grad_x[:, cols] = gradient(gy[:, cols], gn[:, cols], gamma[:, cols], z, scale, inner)

    each_block(one, unroll=4)


class Halving:
    def __init__(self, keep, send, order, own, me, replicas):
        self.keep, self.send, self.order = keep, send, list(order)
        self.left = list(range(replicas.bit_length() - 1))[::-1]
        self.left.remove(self.order[0])
        self.own, self.me, self.replicas = own, me, replicas
        self.came = None

    def go(self):
        bit = self.order.pop(0)
        self.came = lax.ppermute(self.send, "dp", [(i, i ^ (1 << bit)) for i in range(self.replicas)])
        return self

    def add(self):
        if not self.order:
            self.keep, self.send, self.came = self.keep.astype(F32) + self.came.astype(F32), None, None
            return self
        bit = self.order[0]
        place = self.left.index(bit)
        shape = (2**place, 2, 2 ** (len(self.left) - 1 - place) * self.own) + self.keep.shape[1:]
        mine = (self.me >> bit) & 1
        keep, came = self.keep.reshape(shape), self.came.reshape(shape)

        def part(which):
            a = lax.dynamic_index_in_dim(keep, which, 1, keepdims=False)
            b = lax.dynamic_index_in_dim(came, which, 1, keepdims=False)
            total = (a.astype(F32) + b.astype(F32)).astype(self.keep.dtype)
            return total.reshape((shape[0] * shape[2],) + shape[3:])

        self.left.remove(bit)
        self.send, self.keep = part(1 - mine), part(mine)
        self.came = None
        return self

    def finish(self):
        if self.came is not None:
            self.add()
        while self.order:
            self.go().add()
        return self.keep / self.replicas


def met(*halvings, then):
    state = [(h.keep, h.send if h.came is None else h.came) for h in halvings]
    state, then = lax.optimization_barrier((state, then))
    for h, (keep, rest) in zip(halvings, state):
        h.keep = keep
        if h.came is None:
            h.send = rest
        else:
            h.came = rest
    return then


def on_device(replicas, sections, activations, cotangent, token_ids, gains, factors, monarch_perm):
    x = activations[0]
    gamma = gains
    fac = factors[0]
    perm = monarch_perm[0]
    tokens, width = x.shape
    blocks, bs = fac.shape[1], fac.shape[2]
    own = blocks // replicas
    steps = blocks // STEP
    here = lax.axis_index("section")
    me = lax.axis_index("dp")
    live = jnp.broadcast_to((token_ids != 0).astype(F32)[:, None], (tokens, bs))
    flags = jnp.stack([me & 1, (here == sections - 1).astype(jnp.int32)])
    bits = list(range(replicas.bit_length() - 1))
    other = bits[:1] + bits[2:3] + bits[1:2] + bits[3:]

    tok = whole(tokens, width)
    sca = whole(tokens, bs)
    gam = whole(1, width)
    chunk = (STEP * bs, tokens)
    wide = (tokens, STEP * bs)
    fblock = (1, STEP, bs, bs)
    f_at = lambda which: pl.BlockSpec(fblock, lambda c, *_: (which, c, 0, 0))
    c_at = pl.BlockSpec(chunk, lambda c, *_: (c, 0))
    w_at = pl.BlockSpec(wide, lambda c, *_: (0, c))
    g_at = pl.BlockSpec((1, STEP * bs), lambda c, *_: (0, c))
    feat = lambda dt: jax.ShapeDtypeStruct((width, tokens), dt)
    row = lambda dt: jax.ShapeDtypeStruct((tokens, width), dt)
    small = jax.ShapeDtypeStruct((tokens, bs), F32)
    half = lambda n=0, lead=(): jax.ShapeDtypeStruct(lead + (blocks // 2, bs + n, bs), BF16)
    half_at = pl.BlockSpec((STEP // 2, bs, bs), lambda c, *_: (c, 0, 0))
    more_at = pl.BlockSpec((STEP // 2, bs + EXTRA, bs), lambda c, *_: (c, 0, 0))
    two_at = pl.BlockSpec((2, STEP // 2, bs, bs), lambda c, *_: (0, c, 0, 0))
    big = pltpu.VMEM((width, tokens), F32)
    rows = pltpu.VMEM((UNROLL, bs, tokens), F32)
    block = pltpu.VMEM((bs, tokens), F32)
    stage = pltpu.VMEM((2, STEP // 2, bs, bs), BF16)
    part = (steps - 1) * STEP * bs
    last = steps - 1

    def phased(*picks):
        def at(ph, c):
            out = c if picks[-1] is None else picks[-1]
            for i in range(len(picks) - 2, -1, -1):
                out = jnp.where(ph == i, c if picks[i] is None else picks[i], out)
            return out

        return at

    pick = lambda values: lambda ph: jnp.where(ph == 0, values[0], jnp.where(ph == 1, values[1], values[2]))
    a_which, a_at = pick((0, 1, 0)), phased(None, None, None, last)
    b_which, b_at = pick((3, 2, 2)), phased(None, None, last, last)
    cot_at, out_at, mid_at = phased(None, last, last, None), phased(0, 0, 0, None), phased(0, None, last, last)
    mid = pl.BlockSpec(chunk, lambda ph, c, *_: (mid_at(ph, c), 0))
    ap_t, h_t, slope_t, scale, *grad_x = call(
        first_pass,
        "first_pass",
        (4, steps),
        [
            tok,
            pl.BlockSpec(wide, lambda ph, c, *_: (0, cot_at(ph, c))),
            sca,
            gam,
            pl.BlockSpec(fblock, lambda ph, c, *_: (a_which(ph), a_at(ph, c), 0, 0)),
            pl.BlockSpec(fblock, lambda ph, c, *_: (b_which(ph), b_at(ph, c), 0, 0)),
        ],
        [mid, mid, mid, sca, pl.BlockSpec(wide, lambda ph, c, *_: (0, jnp.minimum(out_at(ph, c), last - 1))), whole(*wide)],
        [
            feat(BF16),
            feat(BF16),
            feat(F32),
            small,
            jax.ShapeDtypeStruct((tokens, part), BF16),
            jax.ShapeDtypeStruct(wide, BF16),
        ],
        [big, big, big, pltpu.VMEM((tokens, width), F32), pltpu.VMEM((tokens, bs), F32)] + [block] * 4,
        vmem=50,
    )(perm, x, cotangent, live, gamma, fac, fac)
    moved = [lax.ppermute(piece, "section", [(i, i - 1) for i in range(1, sections)]) for piece in grad_x]

    early, rest = phased(None, last), phased(0, None)
    cp_t = call(
        forward_second,
        "forward_second",
        (2, steps),
        [
            pl.BlockSpec(chunk, lambda ph, c, *_: (early(ph, c), 0)),
            pl.BlockSpec(fblock, lambda ph, c, *_: (2, early(ph, c), 0, 0)),
        ],
        pl.BlockSpec(chunk, lambda ph, c, *_: (rest(ph, c), 0)),
        feat(BF16),
        [big, rows],
    )(perm, h_t, fac)

    start = lambda keep, send, order: Halving(keep, send, order, own, me, replicas)
    shapes = [half(), half(), row(BF16), feat(F32)]
    scratch = [stage, block, block]
    partial = call(
        functools.partial(back_three, own, 0),
        "back_three_early",
        (steps - 1,),
        [w_at, sca, w_at, c_at, f_at(3)],
        [half_at, half_at, w_at, whole(width, tokens)],
        shapes,
        scratch,
        prefetch=2,
    )(perm, flags, cotangent, live, moved[0], cp_t, fac)
    shift = lambda spec: pl.BlockSpec(spec.block_shape, lambda c, *_: spec.index_map(c + last))
    held = pl.BlockSpec(memory_space=pl.ANY)
    partial, moved[1] = lax.optimization_barrier((partial, moved[1]))
    keep, send, gy, gc_t = call(
        functools.partial(back_three, own, steps - 1),
        "back_three_late",
        (1,),
        [shift(w_at), sca, w_at, shift(c_at), shift(f_at(3)), held, held, held, whole(width, tokens)],
        [shift(half_at), shift(half_at), shift(w_at), whole(width, tokens)],
        shapes,
        scratch,
        prefetch=2,
        aliases={7: 0, 8: 1, 9: 2, 10: 3},
    )(perm, flags, cotangent, live, moved[1], cp_t, fac, *partial)
    three = start(keep, send, bits)
    three.go()
    keep_two, send_two, keep_one, send_one, ga_t = call(
        functools.partial(back_two_one, own),
        "back_two_one",
        (steps,),
        [c_at, c_at, c_at, c_at, f_at(2), f_at(1)],
        [half_at] * 4 + [whole(width, tokens)],
        [half()] * 4 + [feat(BF16)],
        [big, stage, stage, block, block],
        prefetch=2,
    )(perm, flags, gc_t, h_t, ap_t, slope_t, fac, fac)
    two, one = start(keep_two, send_two, other), start(keep_one, send_one, bits)
    ga_t, one.keep, one.send, two.keep, two.send = met(three, then=[ga_t, one.keep, one.send, two.keep, two.send])
    three.add()
    (ga_t,) = met(three, then=[ga_t])
    one.go()
    two.go()
    three.go()
    keep_zero, send_zero, gn, inner = call(
        functools.partial(back_zero, own),
        "back_zero",
        (steps,),
        [c_at, w_at, sca, g_at, f_at(0)],
        [more_at, more_at, w_at, sca],
        [half(EXTRA), half(EXTRA), row(F32), small],
        [pltpu.VMEM((tokens, bs), F32)],
    )(flags, ga_t, x, scale, gamma, fac)
    zero = start(keep_zero, send_zero, bits)
    gn, zero.keep, zero.send = met(one, two, then=[gn, zero.keep, zero.send])
    zero.go()
    one.add()
    two.add()
    (gn,) = met(one, two, then=[gn])
    one.go()
    two.go()
    (gn,) = met(zero, three, then=[gn])
    zero.add()
    three.add()
    (gn,) = met(zero, three, then=[gn])
    zero.go()
    three.go()
    out_grad = call(
        back_last,
        "back_last",
        (steps,),
        [w_at, w_at, w_at, sca, g_at, sca],
        w_at,
        row(BF16),
        prefetch=0,
    )(gy, gn, x, scale, gamma, inner)
    (out_grad,) = met(one, two, three, then=[out_grad])
    for each in (one, two, three):
        each.add()
    total = [each.finish() for each in (zero, one, two, three)]
    grad_gamma = total[0][:, bs, :].reshape(1, own * bs)
    total[0] = total[0][:, :bs, :]
    return (out_grad[None], jnp.stack(total)[None], grad_gamma)


def solution(mesh):
    replicas, sections = mesh.shape["dp"], mesh.shape["section"]
    in_specs = (
        P("section", "dp", None),
        P("dp", None),
        P("dp"),
        P("section", None),
        P("section", None, None, None, None),
        P("section", None),
    )
    out_specs = (P("section", "dp", None), P("section", None, "dp", None, None), P("section", "dp"))
    return jax.shard_map(
        functools.partial(on_device, replicas, sections),
        mesh=mesh,
        in_specs=in_specs,
        out_specs=out_specs,
        check_vma=False,
    )
```

```python
import functools

import jax
import jax.numpy as jnp
from jax import lax
from jax.experimental import pallas as pl
from jax.experimental.pallas import tpu as pltpu
from jax.sharding import PartitionSpec as P

F32 = jnp.float32
BF16 = jnp.bfloat16
inv_sqrt_two = 0.7071067811865476
inv_sqrt_two_pi = 0.3989422804014327
STEP = 16
UNROLL = 8
EXTRA = 16


def dot(a, b, ca, cb):
    return lax.dot_general(a, b, (((ca,), (cb,)), ((), ())), preferred_element_type=F32)


def whole(*shape):
    return pl.BlockSpec(shape, lambda *_: (0,) * len(shape))


def call(body, name, grid, in_specs, out_specs, out_shape, scratch=(), prefetch=1, vmem=50, aliases=None):
    return pl.pallas_call(
        body,
        name=name,
        input_output_aliases=aliases or {},
        out_shape=out_shape,
        grid_spec=pltpu.PrefetchScalarGridSpec(
            num_scalar_prefetch=prefetch,
            grid=grid,
            in_specs=in_specs,
            out_specs=out_specs,
            scratch_shapes=scratch,
        ),
        compiler_params=pltpu.CompilerParams(vmem_limit_bytes=vmem << 20),
    )


def each_block(body, count=STEP, unroll=UNROLL):
    def some(i, carry):
        for u in range(unroll):
            body(i * unroll + u, u)
        return carry

    lax.fori_loop(0, count // unroll, some, 0)


def at_block(k, bs):
    return pl.ds(k * bs, bs) if isinstance(k, int) else pl.ds(pl.multiple_of(k * bs, bs), bs)


def rounded(v):
    return v.astype(BF16).astype(F32)


def zed_block(x, scale, cols):
    return x[:, cols].astype(F32) * scale[...]


def gather_rows(perm, base, source, target, count):
    for i in range(count):
        target[pl.ds(i, 1), :] = source[pl.ds(perm[base + i], 1), :]


def scatter_rows(perm, base, source, target, count):
    for i in range(count):
        target[pl.ds(perm[base + i], 1), :] = source[pl.ds(i, 1), :]


def scattered(make, perm, first, target, even, odd, bs):
    def move(k, source):
        scatter_rows(perm, (first + k) * bs, source, target, bs)

    even[...] = make(0)
    for k in range(STEP):
        now, then = (even, odd) if k % 2 == 0 else (odd, even)
        if k + 1 < STEP:
            then[...] = make(k + 1)
        move(k, now)


def gathered_scattered(make, perm, first, source, target, even_in, odd_in, even_out, odd_out, bs):
    def fetch(k, into):
        gather_rows(perm, (first + k) * bs, source, into, bs)

    def move(k, out):
        scatter_rows(perm, (first + k) * bs, out, target, bs)

    for k in range(STEP):
        into, out = (even_in, even_out) if k % 2 == 0 else (odd_in, odd_out)
        fetch(k, into)
        out[...] = make(k, into)
        move(k, out)


def gelu_parts(pre):
    cdf = 0.5 * (1.0 + lax.erf(pre * inv_sqrt_two))
    return (pre * cdf).astype(BF16), cdf + pre * jnp.exp(-0.5 * pre * pre) * inv_sqrt_two_pi


def seeded_block(cot, live, cols):
    return (cot[:, cols].astype(F32) * live[...]).astype(BF16)


def gradient(gy, gn, gamma, z, scale, inner):
    return (gy.astype(F32) + scale[...] * (gn * gamma - z * inner[...])).astype(BF16)


def first_pass(
    perm, x, cot, live, gamma, fac_a, fac_b, ap_t, scale, grad_a, grad_b, a_t, gc_t, ga_t, gn, acc, r0, r1, r2, r3
):
    phase, c = pl.program_id(0), pl.program_id(1)
    bs = fac_a.shape[2]
    blocks = x.shape[1] // bs

    @pl.when(jnp.logical_and(phase == 0, c == 0))
    def _():
        def add(k, total):
            xk = x[:, at_block(k, bs)].astype(F32)
            return total + xk * xk

        total = lax.fori_loop(0, blocks, add, jnp.zeros((x.shape[0], bs), F32), unroll=8)
        mean = jnp.sum(total, axis=1, keepdims=True) / x.shape[1]
        scale[...] = jnp.broadcast_to(lax.rsqrt(mean + 1e-06), scale.shape)
        acc[...] = jnp.zeros(acc.shape, F32)

    @pl.when(phase == 0)
    def _():
        def make(k):
            cols = at_block(c * STEP + k, bs)
            n = (zed_block(x, scale, cols) * gamma[:, cols]).astype(BF16)
            a_t[cols, :] = rounded(dot(fac_a[0, k], n, 0, 1))
            return rounded(dot(fac_b[0, k], seeded_block(cot, live, at_block(k, bs)), 1, 1))

        scattered(make, perm, c * STEP, gc_t, r0, r1, bs)

    @pl.when(phase == 1)
    def _():
        def make(k, rows):
            here = at_block(k, bs)
            ap = rows[...].astype(BF16)
            ap_t[here, :] = ap
            _, slope = gelu_parts(dot(fac_a[0, k], ap, 0, 0))
            gh = dot(fac_b[0, k], gc_t[at_block(c * STEP + k, bs), :].astype(BF16), 1, 0)
            return rounded(dot(fac_a[0, k], (gh * slope).astype(BF16), 1, 0))

        gathered_scattered(make, perm, c * STEP, a_t, ga_t, r0, r1, r2, r3, bs)

    @pl.when(phase == 2)
    def _():
        def one(k, u):
            cols = at_block(c * STEP + k, bs)
            value = dot(ga_t[cols, :].astype(BF16), fac_a[0, k], 0, 1)
            gn[:, cols] = value
            acc[...] += value * gamma[:, cols] * zed_block(x, scale, cols)

        each_block(one)

    @pl.when(jnp.logical_and(phase == 2, c == pl.num_programs(1) - 1))
    def _():
        mean = jnp.sum(acc[...], axis=1, keepdims=True) / x.shape[1]
        acc[...] = jnp.broadcast_to(mean, acc.shape)

    def emit(out):
        def one(k, u):
            here = at_block(k, bs)
            cols = at_block(c * STEP + k, bs)
            z = zed_block(x, scale, cols)
            out[:, here] = gradient(seeded_block(cot, live, here), gn[:, cols], gamma[:, cols], z, scale, acc)

        each_block(one, unroll=4)

    last = pl.num_programs(1) - 1
    pl.when(jnp.logical_and(phase == 3, c < last))(lambda: emit(grad_a))
    pl.when(jnp.logical_and(phase == 3, c == last))(lambda: emit(grad_b))


def forward_second(perm, ap_t, fac_one, fac_two, cp_t, c_t, rows):
    phase, c = pl.program_id(0), pl.program_id(1)
    bs = fac_two.shape[2]

    @pl.when(phase == 0)
    def _():
        def one(k, u):
            h, _ = gelu_parts(dot(fac_one[0, k], ap_t[at_block(k, bs), :], 0, 0))
            c_t[at_block(c * STEP + k, bs), :] = rounded(dot(fac_two[0, k], h, 0, 0))

        each_block(one)

    @pl.when(phase == 1)
    def _():
        def one(k, u):
            gather_rows(perm, (c * STEP + k) * bs, c_t, rows.at[u], bs)
            cp_t[at_block(k, bs), :] = rows[u].astype(BF16)

        each_block(one)


def each_split(flags, own, body):
    for k in range(STEP // 2):
        group, within = divmod(k, own)
        base = group * 2 * own + within
        body(0, k, base + flags[0] * own)
        body(1, k, base + (1 - flags[0]) * own)


def back_three(own, skipped, perm, flags, cot, live, moved, cp_t, fac, *refs):
    *given, keep, send, gy_out, gc_t, even, odd = refs
    bs = fac.shape[2]
    outs = (keep, send)
    if given:
        gc_t[...] = given[3][...]

    def make(k):
        here = at_block(k, bs)
        gy = jnp.where(flags[1] == 1, seeded_block(cot, live, here), moved[:, here])
        gy_out[:, here] = gy
        return rounded(dot(fac[0, k], gy, 1, 1))

    def grads(goes, k, block):
        at = at_block(block, bs)
        outs[goes][k] = dot(cp_t[at, :], gy_out[:, at], 1, 0).astype(BF16)

    scattered(make, perm, (pl.program_id(0) + skipped) * STEP, gc_t, even, odd, bs)
    each_split(flags, own, grads)


def back_two_one(
    own, perm, flags, gc_t, ap_t, fac_two, fac_one, keep_two, send_two, keep_one, send_one, ga_out, ga_t, h_t, gpre_t, gc_b, even, odd
):
    c = pl.program_id(0)
    bs = fac_two.shape[2]
    twos, ones = (keep_two, send_two), (keep_one, send_one)

    def make(k):
        here = at_block(k, bs)
        h_t[here, :], slope = gelu_parts(dot(fac_one[0, k], ap_t[here, :], 0, 0))
        gc = gc_t[here, :].astype(BF16)
        gc_b[here, :] = gc
        gpre = (dot(fac_two[0, k], gc, 1, 0) * slope).astype(BF16)
        gpre_t[here, :] = gpre
        return rounded(dot(fac_one[0, k], gpre, 1, 0))

    def grads(goes, k, block):
        at = at_block(block, bs)
        twos[goes][k] = dot(h_t[at, :], gc_b[at, :], 1, 1).astype(BF16)
        ones[goes][k] = dot(ap_t[at, :], gpre_t[at, :], 1, 1).astype(BF16)

    scattered(make, perm, c * STEP, ga_t, even, odd, bs)
    each_split(flags, own, grads)

    @pl.when(c == pl.num_programs(0) - 1)
    def _():
        ga_out[...] = ga_t[...].astype(BF16)


def back_zero(own, flags, ga_t, x, scale, gamma, fac, keep, send, gn, inner, acc):
    c = pl.program_id(0)
    bs = fac.shape[2]
    outs = (keep, send)

    @pl.when(c == 0)
    def _():
        acc[...] = jnp.zeros(acc.shape, F32)

    def one(goes, k, block):
        at = at_block(block, bs)
        z = zed_block(x, scale, at)
        zg = z * gamma[:, at]
        outs[goes][k, pl.ds(0, bs), :] = dot(zg.astype(BF16), ga_t[at, :], 0, 1).astype(BF16)
        value = dot(ga_t[at, :], fac[0, block], 0, 1)
        gn[:, at] = value
        total = jnp.sum(value * z, axis=0, keepdims=True)
        outs[goes][k, pl.ds(bs, EXTRA), :] = jnp.broadcast_to(total, (EXTRA, bs)).astype(BF16)
        acc[...] += value * zg

    each_split(flags, own, one)

    @pl.when(c == pl.num_programs(0) - 1)
    def _():
        mean = jnp.sum(acc[...], axis=1, keepdims=True) / (x.shape[1] * pl.num_programs(0))
        inner[...] = jnp.broadcast_to(mean, inner.shape)


def back_last(gy, gn, x, scale, gamma, inner, grad_x):
    bs = scale.shape[1]

    def one(k, u):
        cols = at_block(k, bs)
        z = zed_block(x, scale, cols)
        grad_x[:, cols] = gradient(gy[:, cols], gn[:, cols], gamma[:, cols], z, scale, inner)

    each_block(one, unroll=4)


class Halving:
    def __init__(self, keep, send, order, own, me, replicas):
        self.keep, self.send, self.order = keep, send, list(order)
        self.left = list(range(replicas.bit_length() - 1))[::-1]
        self.left.remove(self.order[0])
        self.own, self.me, self.replicas = own, me, replicas
        self.came = None

    def go(self):
        bit = self.order.pop(0)
        self.came = lax.ppermute(self.send, "dp", [(i, i ^ (1 << bit)) for i in range(self.replicas)])
        return self

    def add(self):
        if not self.order:
            self.keep, self.send, self.came = self.keep.astype(F32) + self.came.astype(F32), None, None
            return self
        bit = self.order[0]
        place = self.left.index(bit)
        shape = (2**place, 2, 2 ** (len(self.left) - 1 - place) * self.own) + self.keep.shape[1:]
        mine = (self.me >> bit) & 1
        keep, came = self.keep.reshape(shape), self.came.reshape(shape)

        def part(which):
            a = lax.dynamic_index_in_dim(keep, which, 1, keepdims=False)
            b = lax.dynamic_index_in_dim(came, which, 1, keepdims=False)
            total = (a.astype(F32) + b.astype(F32)).astype(self.keep.dtype)
            return total.reshape((shape[0] * shape[2],) + shape[3:])

        self.left.remove(bit)
        self.send, self.keep = part(1 - mine), part(mine)
        self.came = None
        return self

    def finish(self):
        if self.came is not None:
            self.add()
        while self.order:
            self.go().add()
        return self.keep / self.replicas


def met(*halvings, then):
    state = [(h.keep, h.send if h.came is None else h.came) for h in halvings]
    state, then = lax.optimization_barrier((state, then))
    for h, (keep, rest) in zip(halvings, state):
        h.keep = keep
        if h.came is None:
            h.send = rest
        else:
            h.came = rest
    return then


def on_device(replicas, sections, activations, cotangent, token_ids, gains, factors, monarch_perm):
    x = activations[0]
    gamma = gains
    fac = factors[0]
    perm = monarch_perm[0]
    tokens, width = x.shape
    blocks, bs = fac.shape[1], fac.shape[2]
    own = blocks // replicas
    steps = blocks // STEP
    here = lax.axis_index("section")
    me = lax.axis_index("dp")
    live = jnp.broadcast_to((token_ids != 0).astype(F32)[:, None], (tokens, bs))
    flags = jnp.stack([me & 1, (here == sections - 1).astype(jnp.int32)])
    bits = list(range(replicas.bit_length() - 1))
    other = bits[:1] + bits[2:3] + bits[1:2] + bits[3:]

    tok = whole(tokens, width)
    sca = whole(tokens, bs)
    gam = whole(1, width)
    chunk = (STEP * bs, tokens)
    wide = (tokens, STEP * bs)
    fblock = (1, STEP, bs, bs)
    f_at = lambda which: pl.BlockSpec(fblock, lambda c, *_: (which, c, 0, 0))
    c_at = pl.BlockSpec(chunk, lambda c, *_: (c, 0))
    w_at = pl.BlockSpec(wide, lambda c, *_: (0, c))
    g_at = pl.BlockSpec((1, STEP * bs), lambda c, *_: (0, c))
    feat = lambda dt: jax.ShapeDtypeStruct((width, tokens), dt)
    row = lambda dt: jax.ShapeDtypeStruct((tokens, width), dt)
    small = jax.ShapeDtypeStruct((tokens, bs), F32)
    half = lambda n=0, lead=(): jax.ShapeDtypeStruct(lead + (blocks // 2, bs + n, bs), BF16)
    half_at = pl.BlockSpec((STEP // 2, bs, bs), lambda c, *_: (c, 0, 0))
    more_at = pl.BlockSpec((STEP // 2, bs + EXTRA, bs), lambda c, *_: (c, 0, 0))
    two_at = pl.BlockSpec((2, STEP // 2, bs, bs), lambda c, *_: (0, c, 0, 0))
    big = pltpu.VMEM((width, tokens), F32)
    rows = pltpu.VMEM((UNROLL, bs, tokens), F32)
    block = pltpu.VMEM((bs, tokens), F32)
    part_t = pltpu.VMEM(chunk, BF16)
    part = (steps - 1) * STEP * bs
    last = steps - 1

    def phased(*picks):
        def at(ph, c):
            out = c if picks[-1] is None else picks[-1]
            for i in range(len(picks) - 2, -1, -1):
                out = jnp.where(ph == i, c if picks[i] is None else picks[i], out)
            return out

        return at

    pick = lambda values: lambda ph: jnp.where(ph == 0, values[0], jnp.where(ph == 1, values[1], values[2]))
    a_which, a_at = pick((0, 1, 0)), phased(None, None, None, last)
    b_which, b_at = pick((3, 2, 2)), phased(None, None, last, last)
    cot_at, out_at, mid_at = phased(None, last, last, None), phased(0, 0, 0, None), phased(0, None, last, last)
    mid = pl.BlockSpec(chunk, lambda ph, c, *_: (mid_at(ph, c), 0))
    ap_t, scale, *grad_x = call(
        first_pass,
        "first_pass",
        (4, steps),
        [
            tok,
            pl.BlockSpec(wide, lambda ph, c, *_: (0, cot_at(ph, c))),
            sca,
            gam,
            pl.BlockSpec(fblock, lambda ph, c, *_: (a_which(ph), a_at(ph, c), 0, 0)),
            pl.BlockSpec(fblock, lambda ph, c, *_: (b_which(ph), b_at(ph, c), 0, 0)),
        ],
        [mid, sca, pl.BlockSpec(wide, lambda ph, c, *_: (0, jnp.minimum(out_at(ph, c), last - 1))), whole(*wide)],
        [
            feat(BF16),
            small,
            jax.ShapeDtypeStruct((tokens, part), BF16),
            jax.ShapeDtypeStruct(wide, BF16),
        ],
        [big, big, big, pltpu.VMEM((tokens, width), F32), pltpu.VMEM((tokens, bs), F32)] + [block] * 4,
        vmem=50,
    )(perm, x, cotangent, live, gamma, fac, fac)
    moved = [lax.ppermute(piece, "section", [(i, i - 1) for i in range(1, sections)]) for piece in grad_x]

    early, rest = phased(None, last), phased(0, None)
    cp_t = call(
        forward_second,
        "forward_second",
        (2, steps),
        [
            pl.BlockSpec(chunk, lambda ph, c, *_: (early(ph, c), 0)),
            pl.BlockSpec(fblock, lambda ph, c, *_: (1, early(ph, c), 0, 0)),
            pl.BlockSpec(fblock, lambda ph, c, *_: (2, early(ph, c), 0, 0)),
        ],
        pl.BlockSpec(chunk, lambda ph, c, *_: (rest(ph, c), 0)),
        feat(BF16),
        [big, rows],
    )(perm, ap_t, fac, fac)

    start = lambda keep, send, order: Halving(keep, send, order, own, me, replicas)
    shapes = [half(), half(), row(BF16), feat(F32)]
    scratch = [block, block]
    partial = call(
        functools.partial(back_three, own, 0),
        "back_three_early",
        (steps - 1,),
        [w_at, sca, w_at, c_at, f_at(3)],
        [half_at, half_at, w_at, whole(width, tokens)],
        shapes,
        scratch,
        prefetch=2,
    )(perm, flags, cotangent, live, moved[0], cp_t, fac)
    shift = lambda spec: pl.BlockSpec(spec.block_shape, lambda c, *_: spec.index_map(c + last))
    held = pl.BlockSpec(memory_space=pl.ANY)
    partial, moved[1] = lax.optimization_barrier((partial, moved[1]))
    keep, send, gy, gc_t = call(
        functools.partial(back_three, own, steps - 1),
        "back_three_late",
        (1,),
        [shift(w_at), sca, w_at, shift(c_at), shift(f_at(3)), held, held, held, whole(width, tokens)],
        [shift(half_at), shift(half_at), shift(w_at), whole(width, tokens)],
        shapes,
        scratch,
        prefetch=2,
        aliases={7: 0, 8: 1, 9: 2, 10: 3},
    )(perm, flags, cotangent, live, moved[1], cp_t, fac, *partial)
    three = start(keep, send, bits)
    three.go()
    keep_two, send_two, keep_one, send_one, ga_t = call(
        functools.partial(back_two_one, own),
        "back_two_one",
        (steps,),
        [c_at, c_at, f_at(2), f_at(1)],
        [half_at] * 4 + [whole(width, tokens)],
        [half()] * 4 + [feat(BF16)],
        [big, part_t, part_t, part_t, block, block],
        prefetch=2,
    )(perm, flags, gc_t, ap_t, fac, fac)
    two, one = start(keep_two, send_two, other), start(keep_one, send_one, bits)
    ga_t, one.keep, one.send, two.keep, two.send = met(three, then=[ga_t, one.keep, one.send, two.keep, two.send])
    three.add()
    (ga_t,) = met(three, then=[ga_t])
    one.go()
    two.go()
    three.go()
    keep_zero, send_zero, gn, inner = call(
        functools.partial(back_zero, own),
        "back_zero",
        (steps,),
        [c_at, w_at, sca, g_at, f_at(0)],
        [more_at, more_at, w_at, sca],
        [half(EXTRA), half(EXTRA), row(F32), small],
        [pltpu.VMEM((tokens, bs), F32)],
    )(flags, ga_t, x, scale, gamma, fac)
    zero = start(keep_zero, send_zero, bits)
    gn, zero.keep, zero.send = met(one, two, three, then=[gn, zero.keep, zero.send])
    zero.go()
    for each in (one, two, three):
        each.add()
    (gn,) = met(zero, one, two, three, then=[gn])
    for each in (one, two, three):
        each.go()
    zero.add()
    (gn,) = met(zero, then=[gn])
    zero.go()
    out_grad = call(
        back_last,
        "back_last",
        (steps,),
        [w_at, w_at, w_at, sca, g_at, sca],
        w_at,
        row(BF16),
        prefetch=0,
    )(gy, gn, x, scale, gamma, inner)
    (out_grad,) = met(one, two, three, then=[out_grad])
    for each in (one, two, three):
        each.add()
    total = [each.finish() for each in (zero, one, two, three)]
    grad_gamma = total[0][:, bs, :].reshape(1, own * bs)
    total[0] = total[0][:, :bs, :]
    return (out_grad[None], jnp.stack(total)[None], grad_gamma)


def solution(mesh):
    replicas, sections = mesh.shape["dp"], mesh.shape["section"]
    in_specs = (
        P("section", "dp", None),
        P("dp", None),
        P("dp"),
        P("section", None),
        P("section", None, None, None, None),
        P("section", None),
    )
    out_specs = (P("section", "dp", None), P("section", None, "dp", None, None), P("section", "dp"))
    return jax.shard_map(
        functools.partial(on_device, replicas, sections),
        mesh=mesh,
        in_specs=in_specs,
        out_specs=out_specs,
        check_vma=False,
    )
```

```python
import functools

import jax
import jax.numpy as jnp
from jax import lax
from jax.experimental import pallas as pl
from jax.experimental.pallas import tpu as pltpu
from jax.sharding import PartitionSpec as P

F32 = jnp.float32
BF16 = jnp.bfloat16
inv_sqrt_two = 0.7071067811865476
inv_sqrt_two_pi = 0.3989422804014327
STEP = 16
UNROLL = 8
EXTRA = 16


def dot(a, b, ca, cb):
    return lax.dot_general(a, b, (((ca,), (cb,)), ((), ())), preferred_element_type=F32)


def whole(*shape):
    return pl.BlockSpec(shape, lambda *_: (0,) * len(shape))


def call(body, name, grid, in_specs, out_specs, out_shape, scratch=(), prefetch=1, vmem=50, aliases=None):
    return pl.pallas_call(
        body,
        name=name,
        input_output_aliases=aliases or {},
        out_shape=out_shape,
        grid_spec=pltpu.PrefetchScalarGridSpec(
            num_scalar_prefetch=prefetch,
            grid=grid,
            in_specs=in_specs,
            out_specs=out_specs,
            scratch_shapes=scratch,
        ),
        compiler_params=pltpu.CompilerParams(vmem_limit_bytes=vmem << 20),
    )


def each_block(body, count=STEP, unroll=UNROLL):
    def some(i, carry):
        for u in range(unroll):
            body(i * unroll + u, u)
        return carry

    lax.fori_loop(0, count // unroll, some, 0)


def at_block(k, bs):
    return pl.ds(k * bs, bs) if isinstance(k, int) else pl.ds(pl.multiple_of(k * bs, bs), bs)


def rounded(v):
    return v.astype(BF16).astype(F32)


def zed_block(x, scale, cols):
    return x[:, cols].astype(F32) * scale[...]


def gather_rows(perm, base, source, target, count):
    for i in range(count):
        target[pl.ds(i, 1), :] = source[pl.ds(perm[base + i], 1), :]


def scatter_rows(perm, base, source, target, count):
    for i in range(count):
        target[pl.ds(perm[base + i], 1), :] = source[pl.ds(i, 1), :]


def scattered(make, perm, first, target, even, odd, bs):
    def move(k, source):
        scatter_rows(perm, (first + k) * bs, source, target, bs)

    even[...] = make(0)
    for k in range(STEP):
        now, then = (even, odd) if k % 2 == 0 else (odd, even)
        if k + 1 < STEP:
            then[...] = make(k + 1)
        move(k, now)


def gathered_scattered(make, perm, first, source, target, even_in, odd_in, even_out, odd_out, bs):
    def fetch(k, into):
        gather_rows(perm, (first + k) * bs, source, into, bs)

    def move(k, out):
        scatter_rows(perm, (first + k) * bs, out, target, bs)

    for k in range(STEP):
        into, out = (even_in, even_out) if k % 2 == 0 else (odd_in, odd_out)
        fetch(k, into)
        out[...] = make(k, into)
        move(k, out)


def gelu_parts(pre):
    cdf = 0.5 * (1.0 + lax.erf(pre * inv_sqrt_two))
    return (pre * cdf).astype(BF16), cdf + pre * jnp.exp(-0.5 * pre * pre) * inv_sqrt_two_pi


def seeded_block(cot, live, cols):
    return (cot[:, cols].astype(F32) * live[...]).astype(BF16)


def gradient(gy, gn, gamma, z, scale, inner):
    return (gy.astype(F32) + scale[...] * (gn * gamma - z * inner[...])).astype(BF16)


def first_pass(
    perm, x, cot, live, gamma, fac_a, fac_b, ap_t, scale, grad_a, grad_b, a_t, gc_t, ga_t, gn, acc, r0, r1, r2, r3
):
    phase, c = pl.program_id(0), pl.program_id(1)
    bs = fac_a.shape[2]
    blocks = x.shape[1] // bs

    @pl.when(jnp.logical_and(phase == 0, c == 0))
    def _():
        def add(k, total):
            xk = x[:, at_block(k, bs)].astype(F32)
            return total + xk * xk

        total = lax.fori_loop(0, blocks, add, jnp.zeros((x.shape[0], bs), F32), unroll=8)
        mean = jnp.sum(total, axis=1, keepdims=True) / x.shape[1]
        scale[...] = jnp.broadcast_to(lax.rsqrt(mean + 1e-06), scale.shape)
        acc[...] = jnp.zeros(acc.shape, F32)

    @pl.when(phase == 0)
    def _():
        def make(k):
            cols = at_block(c * STEP + k, bs)
            n = (zed_block(x, scale, cols) * gamma[:, cols]).astype(BF16)
            a_t[cols, :] = rounded(dot(fac_a[0, k], n, 0, 1))
            return rounded(dot(fac_b[0, k], seeded_block(cot, live, at_block(k, bs)), 1, 1))

        scattered(make, perm, c * STEP, gc_t, r0, r1, bs)

    @pl.when(phase == 1)
    def _():
        def make(k, rows):
            here = at_block(k, bs)
            ap = rows[...].astype(BF16)
            ap_t[here, :] = ap
            _, slope = gelu_parts(dot(fac_a[0, k], ap, 0, 0))
            gh = dot(fac_b[0, k], gc_t[at_block(c * STEP + k, bs), :].astype(BF16), 1, 0)
            return rounded(dot(fac_a[0, k], (gh * slope).astype(BF16), 1, 0))

        gathered_scattered(make, perm, c * STEP, a_t, ga_t, r0, r1, r2, r3, bs)

    @pl.when(phase == 2)
    def _():
        def one(k, u):
            cols = at_block(c * STEP + k, bs)
            value = dot(ga_t[cols, :].astype(BF16), fac_a[0, k], 0, 1)
            gn[:, cols] = value
            acc[...] += value * gamma[:, cols] * zed_block(x, scale, cols)

        each_block(one)

    @pl.when(jnp.logical_and(phase == 2, c == pl.num_programs(1) - 1))
    def _():
        mean = jnp.sum(acc[...], axis=1, keepdims=True) / x.shape[1]
        acc[...] = jnp.broadcast_to(mean, acc.shape)

    def emit(out):
        def one(k, u):
            here = at_block(k, bs)
            cols = at_block(c * STEP + k, bs)
            z = zed_block(x, scale, cols)
            out[:, here] = gradient(seeded_block(cot, live, here), gn[:, cols], gamma[:, cols], z, scale, acc)

        each_block(one, unroll=4)

    last = pl.num_programs(1) - 1
    pl.when(jnp.logical_and(phase == 3, c < last))(lambda: emit(grad_a))
    pl.when(jnp.logical_and(phase == 3, c == last))(lambda: emit(grad_b))


def forward_second(perm, ap_t, fac_one, fac_two, cp_t, c_t, rows):
    phase, c = pl.program_id(0), pl.program_id(1)
    bs = fac_two.shape[2]

    @pl.when(phase == 0)
    def _():
        def one(k, u):
            h, _ = gelu_parts(dot(fac_one[0, k], ap_t[at_block(k, bs), :], 0, 0))
            c_t[at_block(c * STEP + k, bs), :] = rounded(dot(fac_two[0, k], h, 0, 0))

        each_block(one)

    @pl.when(phase == 1)
    def _():
        def one(k, u):
            gather_rows(perm, (c * STEP + k) * bs, c_t, rows.at[u], bs)
            cp_t[at_block(k, bs), :] = rows[u].astype(BF16)

        each_block(one)


def each_split(flags, own, body):
    for k in range(STEP // 2):
        group, within = divmod(k, own)
        base = group * 2 * own + within
        body(0, k, base + flags[0] * own)
        body(1, k, base + (1 - flags[0]) * own)


def back_three(own, skipped, perm, flags, cot, live, moved, cp_t, fac, *refs):
    *given, keep, send, gy_out, gc_t, even, odd = refs
    bs = fac.shape[2]
    outs = (keep, send)
    if given:
        gc_t[...] = given[3][...]

    def make(k):
        here = at_block(k, bs)
        gy = jnp.where(flags[1] == 1, seeded_block(cot, live, here), moved[:, here])
        gy_out[:, here] = gy
        return rounded(dot(fac[0, k], gy, 1, 1))

    def grads(goes, k, block):
        at = at_block(block, bs)
        outs[goes][k] = dot(cp_t[at, :], gy_out[:, at], 1, 0).astype(BF16)

    scattered(make, perm, (pl.program_id(0) + skipped) * STEP, gc_t, even, odd, bs)
    each_split(flags, own, grads)


def back_two_one(
    own, perm, flags, gc_t, ap_t, fac_two, fac_one, keep_two, send_two, keep_one, send_one, ga_out, ga_t, h_t, gpre_t, gc_b, even, odd
):
    c = pl.program_id(0)
    bs = fac_two.shape[2]
    twos, ones = (keep_two, send_two), (keep_one, send_one)

    def make(k):
        here = at_block(k, bs)
        h_t[here, :], slope = gelu_parts(dot(fac_one[0, k], ap_t[here, :], 0, 0))
        gc = gc_t[here, :].astype(BF16)
        gc_b[here, :] = gc
        gpre = (dot(fac_two[0, k], gc, 1, 0) * slope).astype(BF16)
        gpre_t[here, :] = gpre
        return rounded(dot(fac_one[0, k], gpre, 1, 0))

    def grads(goes, k, block):
        at = at_block(block, bs)
        twos[goes][k] = dot(h_t[at, :], gc_b[at, :], 1, 1).astype(BF16)
        ones[goes][k] = dot(ap_t[at, :], gpre_t[at, :], 1, 1).astype(BF16)

    scattered(make, perm, c * STEP, ga_t, even, odd, bs)
    each_split(flags, own, grads)

    @pl.when(c == pl.num_programs(0) - 1)
    def _():
        ga_out[...] = ga_t[...].astype(BF16)


def back_zero(own, flags, ga_t, gy, x, scale, gamma, fac, keep, send, grad_x, gn, acc):
    phase, c = pl.program_id(0), pl.program_id(1)
    bs = fac.shape[2]
    outs = (keep, send)

    @pl.when(jnp.logical_and(phase == 0, c == 0))
    def _():
        acc[...] = jnp.zeros(acc.shape, F32)

    @pl.when(phase == 0)
    def _():
        def one(goes, k, block):
            at = at_block(block, bs)
            z = zed_block(x, scale, at)
            zg = z * gamma[:, at]
            outs[goes][k, pl.ds(0, bs), :] = dot(zg.astype(BF16), ga_t[at, :], 0, 1).astype(BF16)
            value = dot(ga_t[at, :], fac[0, block], 0, 1)
            gn[:, at_block(c * STEP + block, bs)] = value
            total = jnp.sum(value * z, axis=0, keepdims=True)
            outs[goes][k, pl.ds(bs, EXTRA), :] = jnp.broadcast_to(total, (EXTRA, bs)).astype(BF16)
            acc[...] += value * zg

        each_split(flags, own, one)

    @pl.when(jnp.logical_and(phase == 0, c == pl.num_programs(1) - 1))
    def _():
        mean = jnp.sum(acc[...], axis=1, keepdims=True) / gn.shape[1]
        acc[...] = jnp.broadcast_to(mean, acc.shape)

    @pl.when(phase == 1)
    def _():
        for k in range(STEP):
            cols = at_block(k, bs)
            z = zed_block(x, scale, cols)
            grad_x[:, cols] = gradient(gy[:, cols], gn[:, at_block(c * STEP + k, bs)], gamma[:, cols], z, scale, acc)


class Halving:
    def __init__(self, keep, send, order, own, me, replicas):
        self.keep, self.send, self.order = keep, send, list(order)
        self.left = list(range(replicas.bit_length() - 1))[::-1]
        self.left.remove(self.order[0])
        self.own, self.me, self.replicas = own, me, replicas
        self.came = None

    def go(self):
        bit = self.order.pop(0)
        self.came = lax.ppermute(self.send, "dp", [(i, i ^ (1 << bit)) for i in range(self.replicas)])
        return self

    def add(self):
        if not self.order:
            self.keep, self.send, self.came = self.keep.astype(F32) + self.came.astype(F32), None, None
            return self
        bit = self.order[0]
        place = self.left.index(bit)
        shape = (2**place, 2, 2 ** (len(self.left) - 1 - place) * self.own) + self.keep.shape[1:]
        mine = (self.me >> bit) & 1
        keep, came = self.keep.reshape(shape), self.came.reshape(shape)

        def part(which):
            a = lax.dynamic_index_in_dim(keep, which, 1, keepdims=False)
            b = lax.dynamic_index_in_dim(came, which, 1, keepdims=False)
            total = (a.astype(F32) + b.astype(F32)).astype(self.keep.dtype)
            return total.reshape((shape[0] * shape[2],) + shape[3:])

        self.left.remove(bit)
        self.send, self.keep = part(1 - mine), part(mine)
        self.came = None
        return self

    def finish(self):
        if self.came is not None:
            self.add()
        while self.order:
            self.go().add()
        return self.keep / self.replicas


def met(*halvings, then):
    state = [(h.keep, h.send if h.came is None else h.came) for h in halvings]
    state, then = lax.optimization_barrier((state, then))
    for h, (keep, rest) in zip(halvings, state):
        h.keep = keep
        if h.came is None:
            h.send = rest
        else:
            h.came = rest
    return then


def behind(first, *others):
    state = [(h.keep, h.came) for h in others]
    first.keep, state = lax.optimization_barrier((first.keep, state))
    for h, (keep, came) in zip(others, state):
        h.keep, h.came = keep, came


def on_device(replicas, sections, activations, cotangent, token_ids, gains, factors, monarch_perm):
    x = activations[0]
    gamma = gains
    fac = factors[0]
    perm = monarch_perm[0]
    tokens, width = x.shape
    blocks, bs = fac.shape[1], fac.shape[2]
    own = blocks // replicas
    steps = blocks // STEP
    here = lax.axis_index("section")
    me = lax.axis_index("dp")
    live = jnp.broadcast_to((token_ids != 0).astype(F32)[:, None], (tokens, bs))
    flags = jnp.stack([me & 1, (here == sections - 1).astype(jnp.int32)])
    bits = list(range(replicas.bit_length() - 1))
    other = bits[:1] + bits[2:3] + bits[1:2] + bits[3:]

    tok = whole(tokens, width)
    sca = whole(tokens, bs)
    gam = whole(1, width)
    chunk = (STEP * bs, tokens)
    wide = (tokens, STEP * bs)
    fblock = (1, STEP, bs, bs)
    f_at = lambda which: pl.BlockSpec(fblock, lambda c, *_: (which, c, 0, 0))
    c_at = pl.BlockSpec(chunk, lambda c, *_: (c, 0))
    w_at = pl.BlockSpec(wide, lambda c, *_: (0, c))
    g_at = pl.BlockSpec((1, STEP * bs), lambda c, *_: (0, c))
    feat = lambda dt: jax.ShapeDtypeStruct((width, tokens), dt)
    row = lambda dt: jax.ShapeDtypeStruct((tokens, width), dt)
    small = jax.ShapeDtypeStruct((tokens, bs), F32)
    half = lambda n=0, lead=(): jax.ShapeDtypeStruct(lead + (blocks // 2, bs + n, bs), BF16)
    half_at = pl.BlockSpec((STEP // 2, bs, bs), lambda c, *_: (c, 0, 0))
    more_at = pl.BlockSpec((STEP // 2, bs + EXTRA, bs), lambda c, *_: (c, 0, 0))
    two_at = pl.BlockSpec((2, STEP // 2, bs, bs), lambda c, *_: (0, c, 0, 0))
    big = pltpu.VMEM((width, tokens), F32)
    rows = pltpu.VMEM((UNROLL, bs, tokens), F32)
    block = pltpu.VMEM((bs, tokens), F32)
    part_t = pltpu.VMEM(chunk, BF16)
    part = (steps - 1) * STEP * bs
    last = steps - 1

    def phased(*picks):
        def at(ph, c):
            out = c if picks[-1] is None else picks[-1]
            for i in range(len(picks) - 2, -1, -1):
                out = jnp.where(ph == i, c if picks[i] is None else picks[i], out)
            return out

        return at

    pick = lambda values: lambda ph: jnp.where(ph == 0, values[0], jnp.where(ph == 1, values[1], values[2]))
    a_which, a_at = pick((0, 1, 0)), phased(None, None, None, last)
    b_which, b_at = pick((3, 2, 2)), phased(None, None, last, last)
    cot_at, out_at, mid_at = phased(None, last, last, None), phased(0, 0, 0, None), phased(0, None, last, last)
    mid = pl.BlockSpec(chunk, lambda ph, c, *_: (mid_at(ph, c), 0))
    ap_t, scale, *grad_x = call(
        first_pass,
        "first_pass",
        (4, steps),
        [
            tok,
            pl.BlockSpec(wide, lambda ph, c, *_: (0, cot_at(ph, c))),
            sca,
            gam,
            pl.BlockSpec(fblock, lambda ph, c, *_: (a_which(ph), a_at(ph, c), 0, 0)),
            pl.BlockSpec(fblock, lambda ph, c, *_: (b_which(ph), b_at(ph, c), 0, 0)),
        ],
        [mid, sca, pl.BlockSpec(wide, lambda ph, c, *_: (0, jnp.minimum(out_at(ph, c), last - 1))), whole(*wide)],
        [
            feat(BF16),
            small,
            jax.ShapeDtypeStruct((tokens, part), BF16),
            jax.ShapeDtypeStruct(wide, BF16),
        ],
        [big, big, big, pltpu.VMEM((tokens, width), F32), pltpu.VMEM((tokens, bs), F32)] + [block] * 4,
        vmem=60,
    )(perm, x, cotangent, live, gamma, fac, fac)
    moved = [lax.ppermute(piece, "section", [(i, i - 1) for i in range(1, sections)]) for piece in grad_x]

    early, rest = phased(None, last), phased(0, None)
    cp_t = call(
        forward_second,
        "forward_second",
        (2, steps),
        [
            pl.BlockSpec(chunk, lambda ph, c, *_: (early(ph, c), 0)),
            pl.BlockSpec(fblock, lambda ph, c, *_: (1, early(ph, c), 0, 0)),
            pl.BlockSpec(fblock, lambda ph, c, *_: (2, early(ph, c), 0, 0)),
        ],
        pl.BlockSpec(chunk, lambda ph, c, *_: (rest(ph, c), 0)),
        feat(BF16),
        [big, rows],
    )(perm, ap_t, fac, fac)

    start = lambda keep, send, order: Halving(keep, send, order, own, me, replicas)
    shapes = [half(), half(), row(BF16), feat(F32)]
    scratch = [block, block]
    partial = call(
        functools.partial(back_three, own, 0),
        "back_three_early",
        (steps - 1,),
        [w_at, sca, w_at, c_at, f_at(3)],
        [half_at, half_at, w_at, whole(width, tokens)],
        shapes,
        scratch,
        prefetch=2,
    )(perm, flags, cotangent, live, moved[0], cp_t, fac)
    shift = lambda spec: pl.BlockSpec(spec.block_shape, lambda c, *_: spec.index_map(c + last))
    held = pl.BlockSpec(memory_space=pl.ANY)
    partial, moved[1] = lax.optimization_barrier((partial, moved[1]))
    keep, send, gy, gc_t = call(
        functools.partial(back_three, own, steps - 1),
        "back_three_late",
        (1,),
        [shift(w_at), sca, w_at, shift(c_at), shift(f_at(3)), held, held, held, whole(width, tokens)],
        [shift(half_at), shift(half_at), shift(w_at), whole(width, tokens)],
        shapes,
        scratch,
        prefetch=2,
        aliases={7: 0, 8: 1, 9: 2, 10: 3},
    )(perm, flags, cotangent, live, moved[1], cp_t, fac, *partial)
    three = start(keep, send, bits)
    three.go()
    keep_two, send_two, keep_one, send_one, ga_t = call(
        functools.partial(back_two_one, own),
        "back_two_one",
        (steps,),
        [c_at, c_at, f_at(2), f_at(1)],
        [half_at] * 4 + [whole(width, tokens)],
        [half()] * 4 + [feat(BF16)],
        [big, part_t, part_t, part_t, block, block],
        prefetch=2,
    )(perm, flags, gc_t, ap_t, fac, fac)
    two, one = start(keep_two, send_two, other), start(keep_one, send_one, bits)
    ga_t, one.keep, one.send, two.keep, two.send = met(three, then=[ga_t, one.keep, one.send, two.keep, two.send])
    three.add()
    (ga_t,) = met(three, then=[ga_t])
    one.go()
    two.go()
    three.go()
    held_at = lambda shape, at, *lead: pl.BlockSpec(shape, lambda ph, c, *_: lead + (at(ph, c),) + (0,) * (len(shape) - 1 - len(lead)))
    across = lambda shape, at: pl.BlockSpec(shape, lambda ph, c, *_: (0, at(ph, c)))
    both = phased(None, None)
    keep_zero, send_zero, out_grad = call(
        functools.partial(back_zero, own),
        "back_zero",
        (2, steps),
        [
            held_at(chunk, early),
            across(wide, rest),
            across(wide, both),
            sca,
            across((1, STEP * bs), both),
            held_at(fblock, early, 0),
        ],
        [held_at(more_at.block_shape, early)] * 2 + [across(wide, rest)],
        [half(EXTRA), half(EXTRA), row(BF16)],
        [pltpu.VMEM((tokens, width), F32), pltpu.VMEM((tokens, bs), F32)],
    )(flags, ga_t, gy, x, scale, gamma, fac)
    zero = start(keep_zero, send_zero, bits)
    out_grad, zero.keep, zero.send = met(one, two, three, then=[out_grad, zero.keep, zero.send])
    zero.go()
    one.add().go()
    zero.add().go()
    two.add().go()
    three.add().go()
    one.add().go()
    zero.add().go()
    behind(zero, one, two)
    total = [each.finish() for each in (zero, one, two, three)]
    grad_gamma = total[0][:, bs, :].reshape(1, own * bs)
    total[0] = total[0][:, :bs, :]
    return (out_grad[None], jnp.stack(total)[None], grad_gamma)


def solution(mesh):
    replicas, sections = mesh.shape["dp"], mesh.shape["section"]
    in_specs = (
        P("section", "dp", None),
        P("dp", None),
        P("dp"),
        P("section", None),
        P("section", None, None, None, None),
        P("section", None),
    )
    out_specs = (P("section", "dp", None), P("section", None, "dp", None, None), P("section", "dp"))
    return jax.shard_map(
        functools.partial(on_device, replicas, sections),
        mesh=mesh,
        in_specs=in_specs,
        out_specs=out_specs,
        check_vma=False,
    )
```

```python
import functools

import jax
import jax.numpy as jnp
from jax import lax
from jax.experimental import pallas as pl
from jax.experimental.pallas import tpu as pltpu
from jax.sharding import PartitionSpec as P

F32 = jnp.float32
BF16 = jnp.bfloat16
inv_sqrt_two = 0.7071067811865476
inv_sqrt_two_pi = 0.3989422804014327
STEP = 16
UNROLL = 8
EXTRA = 16


def dot(a, b, ca, cb):
    return lax.dot_general(a, b, (((ca,), (cb,)), ((), ())), preferred_element_type=F32)


def whole(*shape):
    return pl.BlockSpec(shape, lambda *_: (0,) * len(shape))


def call(body, name, grid, in_specs, out_specs, out_shape, scratch=(), prefetch=1, vmem=50, aliases=None):
    return pl.pallas_call(
        body,
        name=name,
        input_output_aliases=aliases or {},
        out_shape=out_shape,
        grid_spec=pltpu.PrefetchScalarGridSpec(
            num_scalar_prefetch=prefetch,
            grid=grid,
            in_specs=in_specs,
            out_specs=out_specs,
            scratch_shapes=scratch,
        ),
        compiler_params=pltpu.CompilerParams(vmem_limit_bytes=vmem << 20),
    )


def each_block(body, count=STEP, unroll=UNROLL):
    def some(i, carry):
        for u in range(unroll):
            body(i * unroll + u, u)
        return carry

    lax.fori_loop(0, count // unroll, some, 0)


def at_block(k, bs):
    return pl.ds(k * bs, bs) if isinstance(k, int) else pl.ds(pl.multiple_of(k * bs, bs), bs)


def rounded(v):
    return v.astype(BF16).astype(F32)


def zed_block(x, scale, cols):
    return x[:, cols].astype(F32) * scale[...]


def gather_rows(perm, base, source, target, count):
    for i in range(count):
        target[pl.ds(i, 1), :] = source[pl.ds(perm[base + i], 1), :]


def scatter_rows(perm, base, source, target, count):
    for i in range(count):
        target[pl.ds(perm[base + i], 1), :] = source[pl.ds(i, 1), :]


def scattered(make, perm, first, target, even, odd, bs):
    def move(k, source):
        scatter_rows(perm, (first + k) * bs, source, target, bs)

    even[...] = make(0)
    for k in range(STEP):
        now, then = (even, odd) if k % 2 == 0 else (odd, even)
        if k + 1 < STEP:
            then[...] = make(k + 1)
        move(k, now)


def gathered_scattered(make, perm, first, source, target, even_in, odd_in, even_out, odd_out, bs):
    def fetch(k, into):
        gather_rows(perm, (first + k) * bs, source, into, bs)

    def move(k, out):
        scatter_rows(perm, (first + k) * bs, out, target, bs)

    for k in range(STEP):
        into, out = (even_in, even_out) if k % 2 == 0 else (odd_in, odd_out)
        fetch(k, into)
        out[...] = make(k, into)
        move(k, out)


def gelu_parts(pre):
    cdf = 0.5 * (1.0 + lax.erf(pre * inv_sqrt_two))
    return (pre * cdf).astype(BF16), cdf + pre * jnp.exp(-0.5 * pre * pre) * inv_sqrt_two_pi


def seeded_block(cot, live, cols):
    return (cot[:, cols].astype(F32) * live[...]).astype(BF16)


def gradient(gy, gn, gamma, z, scale, inner):
    return (gy.astype(F32) + scale[...] * (gn * gamma - z * inner[...])).astype(BF16)


def first_pass(
    perm, x, cot, live, gamma, fac_a, fac_b, ap_t, scale, grad_a, grad_b, a_t, gc_t, ga_t, gn, acc, r0, r1, r2, r3
):
    phase, c = pl.program_id(0), pl.program_id(1)
    bs = fac_a.shape[2]
    blocks = x.shape[1] // bs

    @pl.when(jnp.logical_and(phase == 0, c == 0))
    def _():
        def add(k, total):
            xk = x[:, at_block(k, bs)].astype(F32)
            return total + xk * xk

        total = lax.fori_loop(0, blocks, add, jnp.zeros((x.shape[0], bs), F32), unroll=8)
        mean = jnp.sum(total, axis=1, keepdims=True) / x.shape[1]
        scale[...] = jnp.broadcast_to(lax.rsqrt(mean + 1e-06), scale.shape)
        acc[...] = jnp.zeros(acc.shape, F32)

    @pl.when(phase == 0)
    def _():
        def make(k):
            cols = at_block(c * STEP + k, bs)
            n = (zed_block(x, scale, cols) * gamma[:, cols]).astype(BF16)
            a_t[cols, :] = rounded(dot(fac_a[0, k], n, 0, 1))
            return rounded(dot(fac_b[0, k], seeded_block(cot, live, at_block(k, bs)), 1, 1))

        scattered(make, perm, c * STEP, gc_t, r0, r1, bs)

    @pl.when(phase == 1)
    def _():
        def make(k, rows):
            here = at_block(k, bs)
            ap = rows[...].astype(BF16)
            ap_t[here, :] = ap
            _, slope = gelu_parts(dot(fac_a[0, k], ap, 0, 0))
            gh = dot(fac_b[0, k], gc_t[at_block(c * STEP + k, bs), :].astype(BF16), 1, 0)
            return rounded(dot(fac_a[0, k], (gh * slope).astype(BF16), 1, 0))

        gathered_scattered(make, perm, c * STEP, a_t, ga_t, r0, r1, r2, r3, bs)

    @pl.when(phase == 2)
    def _():
        def one(k, u):
            cols = at_block(c * STEP + k, bs)
            value = dot(ga_t[cols, :].astype(BF16), fac_a[0, k], 0, 1)
            gn[:, cols] = value
            acc[...] += value * gamma[:, cols] * zed_block(x, scale, cols)

        each_block(one)

    @pl.when(jnp.logical_and(phase == 2, c == pl.num_programs(1) - 1))
    def _():
        mean = jnp.sum(acc[...], axis=1, keepdims=True) / x.shape[1]
        acc[...] = jnp.broadcast_to(mean, acc.shape)

    def emit(out):
        def one(k, u):
            here = at_block(k, bs)
            cols = at_block(c * STEP + k, bs)
            z = zed_block(x, scale, cols)
            out[:, here] = gradient(seeded_block(cot, live, here), gn[:, cols], gamma[:, cols], z, scale, acc)

        each_block(one, unroll=4)

    last = pl.num_programs(1) - 1
    pl.when(jnp.logical_and(phase == 3, c < last))(lambda: emit(grad_a))
    pl.when(jnp.logical_and(phase == 3, c == last))(lambda: emit(grad_b))


def forward_second(perm, ap_t, fac_one, fac_two, cp_t, c_t, rows):
    phase, c = pl.program_id(0), pl.program_id(1)
    bs = fac_two.shape[2]

    @pl.when(phase == 0)
    def _():
        def one(k, u):
            h, _ = gelu_parts(dot(fac_one[0, k], ap_t[at_block(k, bs), :], 0, 0))
            c_t[at_block(c * STEP + k, bs), :] = rounded(dot(fac_two[0, k], h, 0, 0))

        each_block(one)

    @pl.when(phase == 1)
    def _():
        def one(k, u):
            gather_rows(perm, (c * STEP + k) * bs, c_t, rows.at[u], bs)
            cp_t[at_block(k, bs), :] = rows[u].astype(BF16)

        each_block(one)


def each_split(flags, own, body):
    for k in range(STEP // 2):
        group, within = divmod(k, own)
        base = group * 2 * own + within
        body(0, k, base + flags[0] * own)
        body(1, k, base + (1 - flags[0]) * own)


def back_three(own, skipped, perm, flags, cot, live, moved, cp_t, fac, *refs):
    if len(refs) > 6:
        _, _, _, gc_in, keep, send, gy_out, gc_out, gc_t, even, odd = refs
        gc_t[...] = gc_in[...]
    else:
        keep, send, gy_out, gc_t, even, odd = refs
        gc_out = None
    bs = fac.shape[2]
    outs = (keep, send)

    def make(k):
        here = at_block(k, bs)
        gy = jnp.where(flags[1] == 1, seeded_block(cot, live, here), moved[:, here])
        gy_out[:, here] = gy
        return rounded(dot(fac[0, k], gy, 1, 1))

    def grads(goes, k, block):
        at = at_block(block, bs)
        outs[goes][k] = dot(cp_t[at, :], gy_out[:, at], 1, 0).astype(BF16)

    scattered(make, perm, (pl.program_id(0) + skipped) * STEP, gc_t, even, odd, bs)
    each_split(flags, own, grads)
    if gc_out is not None:
        gc_out[...] = gc_t[...].astype(BF16)


def back_two_one(
    own, perm, flags, gc_t, ap_t, fac_two, fac_one, keep_two, send_two, keep_one, send_one, ga_out, ga_t, h_t, gpre_t, even, odd
):
    c = pl.program_id(0)
    bs = fac_two.shape[2]
    twos, ones = (keep_two, send_two), (keep_one, send_one)

    def make(k):
        here = at_block(k, bs)
        h_t[here, :], slope = gelu_parts(dot(fac_one[0, k], ap_t[here, :], 0, 0))
        gpre = (dot(fac_two[0, k], gc_t[here, :], 1, 0) * slope).astype(BF16)
        gpre_t[here, :] = gpre
        return rounded(dot(fac_one[0, k], gpre, 1, 0))

    def grads(goes, k, block):
        at = at_block(block, bs)
        twos[goes][k] = dot(h_t[at, :], gc_t[at, :], 1, 1).astype(BF16)
        ones[goes][k] = dot(ap_t[at, :], gpre_t[at, :], 1, 1).astype(BF16)

    scattered(make, perm, c * STEP, ga_t, even, odd, bs)
    each_split(flags, own, grads)

    @pl.when(c == pl.num_programs(0) - 1)
    def _():
        ga_out[...] = ga_t[...].astype(BF16)


def back_zero(own, flags, ga_t, gy, x, scale, gamma, fac, keep, send, grad_x, gn, acc):
    phase, c = pl.program_id(0), pl.program_id(1)
    bs = fac.shape[2]
    outs = (keep, send)

    @pl.when(jnp.logical_and(phase == 0, c == 0))
    def _():
        acc[...] = jnp.zeros(acc.shape, F32)

    @pl.when(phase == 0)
    def _():
        def one(goes, k, block):
            at = at_block(block, bs)
            z = zed_block(x, scale, at)
            zg = z * gamma[:, at]
            outs[goes][k, pl.ds(0, bs), :] = dot(zg.astype(BF16), ga_t[at, :], 0, 1).astype(BF16)
            value = dot(ga_t[at, :], fac[0, block], 0, 1)
            gn[:, at_block(c * STEP + block, bs)] = value
            total = jnp.sum(value * z, axis=0, keepdims=True)
            outs[goes][k, pl.ds(bs, EXTRA), :] = jnp.broadcast_to(total, (EXTRA, bs)).astype(BF16)
            acc[...] += value * zg

        each_split(flags, own, one)

    @pl.when(jnp.logical_and(phase == 0, c == pl.num_programs(1) - 1))
    def _():
        mean = jnp.sum(acc[...], axis=1, keepdims=True) / gn.shape[1]
        acc[...] = jnp.broadcast_to(mean, acc.shape)

    @pl.when(phase == 1)
    def _():
        for k in range(STEP):
            cols = at_block(k, bs)
            z = zed_block(x, scale, cols)
            grad_x[:, cols] = gradient(gy[:, cols], gn[:, at_block(c * STEP + k, bs)], gamma[:, cols], z, scale, acc)


class Halving:
    def __init__(self, keep, send, order, own, me, replicas):
        self.keep, self.send, self.order = keep, send, list(order)
        self.left = list(range(replicas.bit_length() - 1))[::-1]
        self.left.remove(self.order[0])
        self.own, self.me, self.replicas = own, me, replicas
        self.came = None

    def go(self):
        bit = self.order.pop(0)
        self.came = lax.ppermute(self.send, "dp", [(i, i ^ (1 << bit)) for i in range(self.replicas)])
        return self

    def add(self):
        if not self.order:
            self.keep, self.send, self.came = self.keep.astype(F32) + self.came.astype(F32), None, None
            return self
        bit = self.order[0]
        place = self.left.index(bit)
        shape = (2**place, 2, 2 ** (len(self.left) - 1 - place) * self.own) + self.keep.shape[1:]
        mine = (self.me >> bit) & 1
        keep, came = self.keep.reshape(shape), self.came.reshape(shape)

        def part(which):
            a = lax.dynamic_index_in_dim(keep, which, 1, keepdims=False)
            b = lax.dynamic_index_in_dim(came, which, 1, keepdims=False)
            total = (a.astype(F32) + b.astype(F32)).astype(self.keep.dtype)
            return total.reshape((shape[0] * shape[2],) + shape[3:])

        self.left.remove(bit)
        self.send, self.keep = part(1 - mine), part(mine)
        self.came = None
        return self

    def finish(self):
        if self.came is not None:
            self.add()
        while self.order:
            self.go().add()
        return self.keep / self.replicas


def met(*halvings, then):
    state = [(h.keep, h.send if h.came is None else h.came) for h in halvings]
    state, then = lax.optimization_barrier((state, then))
    for h, (keep, rest) in zip(halvings, state):
        h.keep = keep
        if h.came is None:
            h.send = rest
        else:
            h.came = rest
    return then


def behind(first, *others):
    state = [(h.keep, h.came) for h in others]
    first.keep, state = lax.optimization_barrier((first.keep, state))
    for h, (keep, came) in zip(others, state):
        h.keep, h.came = keep, came


def on_device(replicas, sections, activations, cotangent, token_ids, gains, factors, monarch_perm):
    x = activations[0]
    gamma = gains
    fac = factors[0]
    perm = monarch_perm[0]
    tokens, width = x.shape
    blocks, bs = fac.shape[1], fac.shape[2]
    own = blocks // replicas
    steps = blocks // STEP
    here = lax.axis_index("section")
    me = lax.axis_index("dp")
    live = jnp.broadcast_to((token_ids != 0).astype(F32)[:, None], (tokens, bs))
    flags = jnp.stack([me & 1, (here == sections - 1).astype(jnp.int32)])
    bits = list(range(replicas.bit_length() - 1))
    other = bits[:1] + bits[2:3] + bits[1:2] + bits[3:]

    tok = whole(tokens, width)
    sca = whole(tokens, bs)
    gam = whole(1, width)
    chunk = (STEP * bs, tokens)
    wide = (tokens, STEP * bs)
    fblock = (1, STEP, bs, bs)
    f_at = lambda which: pl.BlockSpec(fblock, lambda c, *_: (which, c, 0, 0))
    c_at = pl.BlockSpec(chunk, lambda c, *_: (c, 0))
    w_at = pl.BlockSpec(wide, lambda c, *_: (0, c))
    g_at = pl.BlockSpec((1, STEP * bs), lambda c, *_: (0, c))
    feat = lambda dt: jax.ShapeDtypeStruct((width, tokens), dt)
    row = lambda dt: jax.ShapeDtypeStruct((tokens, width), dt)
    small = jax.ShapeDtypeStruct((tokens, bs), F32)
    half = lambda n=0, lead=(): jax.ShapeDtypeStruct(lead + (blocks // 2, bs + n, bs), BF16)
    half_at = pl.BlockSpec((STEP // 2, bs, bs), lambda c, *_: (c, 0, 0))
    more_at = pl.BlockSpec((STEP // 2, bs + EXTRA, bs), lambda c, *_: (c, 0, 0))
    two_at = pl.BlockSpec((2, STEP // 2, bs, bs), lambda c, *_: (0, c, 0, 0))
    big = pltpu.VMEM((width, tokens), F32)
    rows = pltpu.VMEM((UNROLL, bs, tokens), F32)
    block = pltpu.VMEM((bs, tokens), F32)
    part_t = pltpu.VMEM(chunk, BF16)
    part = (steps - 1) * STEP * bs
    last = steps - 1

    def phased(*picks):
        def at(ph, c):
            out = c if picks[-1] is None else picks[-1]
            for i in range(len(picks) - 2, -1, -1):
                out = jnp.where(ph == i, c if picks[i] is None else picks[i], out)
            return out

        return at

    pick = lambda values: lambda ph: jnp.where(ph == 0, values[0], jnp.where(ph == 1, values[1], values[2]))
    a_which, a_at = pick((0, 1, 0)), phased(None, None, None, last)
    b_which, b_at = pick((3, 2, 2)), phased(None, None, last, last)
    cot_at, out_at, mid_at = phased(None, last, last, None), phased(0, 0, 0, None), phased(0, None, last, last)
    mid = pl.BlockSpec(chunk, lambda ph, c, *_: (mid_at(ph, c), 0))
    ap_t, scale, *grad_x = call(
        first_pass,
        "first_pass",
        (4, steps),
        [
            tok,
            pl.BlockSpec(wide, lambda ph, c, *_: (0, cot_at(ph, c))),
            sca,
            gam,
            pl.BlockSpec(fblock, lambda ph, c, *_: (a_which(ph), a_at(ph, c), 0, 0)),
            pl.BlockSpec(fblock, lambda ph, c, *_: (b_which(ph), b_at(ph, c), 0, 0)),
        ],
        [mid, sca, pl.BlockSpec(wide, lambda ph, c, *_: (0, jnp.minimum(out_at(ph, c), last - 1))), whole(*wide)],
        [
            feat(BF16),
            small,
            jax.ShapeDtypeStruct((tokens, part), BF16),
            jax.ShapeDtypeStruct(wide, BF16),
        ],
        [big, big, big, pltpu.VMEM((tokens, width), F32), pltpu.VMEM((tokens, bs), F32)] + [block] * 4,
        vmem=60,
    )(perm, x, cotangent, live, gamma, fac, fac)
    moved = [lax.ppermute(piece, "section", [(i, i - 1) for i in range(1, sections)]) for piece in grad_x]

    early, rest = phased(None, last), phased(0, None)
    cp_t = call(
        forward_second,
        "forward_second",
        (2, steps),
        [
            pl.BlockSpec(chunk, lambda ph, c, *_: (early(ph, c), 0)),
            pl.BlockSpec(fblock, lambda ph, c, *_: (1, early(ph, c), 0, 0)),
            pl.BlockSpec(fblock, lambda ph, c, *_: (2, early(ph, c), 0, 0)),
        ],
        pl.BlockSpec(chunk, lambda ph, c, *_: (rest(ph, c), 0)),
        feat(BF16),
        [big, rows],
    )(perm, ap_t, fac, fac)

    start = lambda keep, send, order: Halving(keep, send, order, own, me, replicas)
    shapes = [half(), half(), row(BF16), feat(F32)]
    scratch = [block, block]
    partial = call(
        functools.partial(back_three, own, 0),
        "back_three_early",
        (steps - 1,),
        [w_at, sca, w_at, c_at, f_at(3)],
        [half_at, half_at, w_at, whole(width, tokens)],
        shapes,
        scratch,
        prefetch=2,
    )(perm, flags, cotangent, live, moved[0], cp_t, fac)
    shift = lambda spec: pl.BlockSpec(spec.block_shape, lambda c, *_: spec.index_map(c + last))
    held = pl.BlockSpec(memory_space=pl.ANY)
    partial, moved[1] = lax.optimization_barrier((partial, moved[1]))
    keep, send, gy, gc_t = call(
        functools.partial(back_three, own, steps - 1),
        "back_three_late",
        (1,),
        [shift(w_at), sca, w_at, shift(c_at), shift(f_at(3)), held, held, held, whole(width, tokens)],
        [shift(half_at), shift(half_at), shift(w_at), whole(width, tokens)],
        shapes[:3] + [feat(BF16)],
        [big] + scratch,
        prefetch=2,
        aliases={7: 0, 8: 1, 9: 2},
    )(perm, flags, cotangent, live, moved[1], cp_t, fac, *partial)
    three = start(keep, send, bits)
    three.go()
    keep_two, send_two, keep_one, send_one, ga_t = call(
        functools.partial(back_two_one, own),
        "back_two_one",
        (steps,),
        [c_at, c_at, f_at(2), f_at(1)],
        [half_at] * 4 + [whole(width, tokens)],
        [half()] * 4 + [feat(BF16)],
        [big, part_t, part_t, block, block],
        prefetch=2,
    )(perm, flags, gc_t, ap_t, fac, fac)
    two, one = start(keep_two, send_two, other), start(keep_one, send_one, bits)
    ga_t, one.keep, one.send, two.keep, two.send = met(three, then=[ga_t, one.keep, one.send, two.keep, two.send])
    three.add()
    (ga_t,) = met(three, then=[ga_t])
    one.go()
    two.go()
    three.go()
    held_at = lambda shape, at, *lead: pl.BlockSpec(shape, lambda ph, c, *_: lead + (at(ph, c),) + (0,) * (len(shape) - 1 - len(lead)))
    across = lambda shape, at: pl.BlockSpec(shape, lambda ph, c, *_: (0, at(ph, c)))
    both = phased(None, None)
    keep_zero, send_zero, out_grad = call(
        functools.partial(back_zero, own),
        "back_zero",
        (2, steps),
        [
            held_at(chunk, early),
            across(wide, rest),
            across(wide, both),
            sca,
            across((1, STEP * bs), both),
            held_at(fblock, early, 0),
        ],
        [held_at(more_at.block_shape, early)] * 2 + [across(wide, rest)],
        [half(EXTRA), half(EXTRA), row(BF16)],
        [pltpu.VMEM((tokens, width), F32), pltpu.VMEM((tokens, bs), F32)],
    )(flags, ga_t, gy, x, scale, gamma, fac)
    zero = start(keep_zero, send_zero, bits)
    out_grad, zero.keep, zero.send = met(one, two, three, then=[out_grad, zero.keep, zero.send])
    zero.go()
    one.add().go()
    zero.add().go()
    two.add().go()
    three.add().go()
    one.add().go()
    zero.add().go()
    behind(zero, one, two)
    total = [each.finish() for each in (zero, one, two, three)]
    grad_gamma = total[0][:, bs, :].reshape(1, own * bs)
    total[0] = total[0][:, :bs, :]
    return (out_grad[None], jnp.stack(total)[None], grad_gamma)


def solution(mesh):
    replicas, sections = mesh.shape["dp"], mesh.shape["section"]
    in_specs = (
        P("section", "dp", None),
        P("dp", None),
        P("dp"),
        P("section", None),
        P("section", None, None, None, None),
        P("section", None),
    )
    out_specs = (P("section", "dp", None), P("section", None, "dp", None, None), P("section", "dp"))
    return jax.shard_map(
        functools.partial(on_device, replicas, sections),
        mesh=mesh,
        in_specs=in_specs,
        out_specs=out_specs,
        check_vma=False,
    )
```

```python
import functools

import jax
import jax.numpy as jnp
from jax import lax
from jax.experimental import pallas as pl
from jax.experimental.pallas import tpu as pltpu
from jax.sharding import PartitionSpec as P

F32 = jnp.float32
BF16 = jnp.bfloat16
inv_sqrt_two = 0.7071067811865476
inv_sqrt_two_pi = 0.3989422804014327
STEP = 16
UNROLL = 8
EXTRA = 16


def dot(a, b, ca, cb):
    return lax.dot_general(a, b, (((ca,), (cb,)), ((), ())), preferred_element_type=F32)


def whole(*shape):
    return pl.BlockSpec(shape, lambda *_: (0,) * len(shape))


def call(body, name, grid, in_specs, out_specs, out_shape, scratch=(), prefetch=1, vmem=50, aliases=None):
    return pl.pallas_call(
        body,
        name=name,
        input_output_aliases=aliases or {},
        out_shape=out_shape,
        grid_spec=pltpu.PrefetchScalarGridSpec(
            num_scalar_prefetch=prefetch,
            grid=grid,
            in_specs=in_specs,
            out_specs=out_specs,
            scratch_shapes=scratch,
        ),
        compiler_params=pltpu.CompilerParams(vmem_limit_bytes=vmem << 20),
    )


def each_block(body, count=STEP, unroll=UNROLL):
    def some(i, carry):
        for u in range(unroll):
            body(i * unroll + u, u)
        return carry

    lax.fori_loop(0, count // unroll, some, 0)


def at_block(k, bs):
    return pl.ds(k * bs, bs) if isinstance(k, int) else pl.ds(pl.multiple_of(k * bs, bs), bs)


def rounded(v):
    return v.astype(BF16).astype(F32)


def zed_block(x, scale, cols):
    return x[:, cols].astype(F32) * scale[...]


def gather_rows(perm, base, source, target, count):
    for i in range(count):
        target[pl.ds(i, 1), :] = source[pl.ds(perm[base + i], 1), :]


def scatter_rows(perm, base, source, target, count):
    for i in range(count):
        target[pl.ds(perm[base + i], 1), :] = source[pl.ds(i, 1), :]


def scattered(make, perm, first, target, even, odd, bs):
    def move(k, source):
        scatter_rows(perm, (first + k) * bs, source, target, bs)

    even[...] = make(0)
    for k in range(STEP):
        now, then = (even, odd) if k % 2 == 0 else (odd, even)
        if k + 1 < STEP:
            then[...] = make(k + 1)
        move(k, now)


def gathered_scattered(make, perm, first, source, target, even_in, odd_in, even_out, odd_out, bs):
    def fetch(k, into):
        gather_rows(perm, (first + k) * bs, source, into, bs)

    def move(k, out):
        scatter_rows(perm, (first + k) * bs, out, target, bs)

    for k in range(STEP):
        into, out = (even_in, even_out) if k % 2 == 0 else (odd_in, odd_out)
        fetch(k, into)
        out[...] = make(k, into)
        move(k, out)


def gelu_parts(pre):
    cdf = 0.5 * (1.0 + lax.erf(pre * inv_sqrt_two))
    return (pre * cdf).astype(BF16), cdf + pre * jnp.exp(-0.5 * pre * pre) * inv_sqrt_two_pi


def seeded_block(cot, live, cols):
    return (cot[:, cols].astype(F32) * live[...]).astype(BF16)


def gradient(gy, gn, gamma, z, scale, inner):
    return (gy.astype(F32) + scale[...] * (gn * gamma - z * inner[...])).astype(BF16)


def first_pass(
    perm, x, cot, live, gamma, fac_a, fac_b, ap_t, scale, grad_a, grad_b, a_t, gc_t, ga_t, gn, acc, r0, r1, r2, r3
):
    phase, c = pl.program_id(0), pl.program_id(1)
    bs = fac_a.shape[2]
    blocks = x.shape[1] // bs

    @pl.when(jnp.logical_and(phase == 0, c == 0))
    def _():
        def add(k, total):
            xk = x[:, at_block(k, bs)].astype(F32)
            return total + xk * xk

        total = lax.fori_loop(0, blocks, add, jnp.zeros((x.shape[0], bs), F32), unroll=8)
        mean = jnp.sum(total, axis=1, keepdims=True) / x.shape[1]
        scale[...] = jnp.broadcast_to(lax.rsqrt(mean + 1e-06), scale.shape)
        acc[...] = jnp.zeros(acc.shape, F32)

    @pl.when(phase == 0)
    def _():
        def make(k):
            cols = at_block(c * STEP + k, bs)
            n = (zed_block(x, scale, cols) * gamma[:, cols]).astype(BF16)
            a_t[cols, :] = rounded(dot(fac_a[0, k], n, 0, 1))
            return rounded(dot(fac_b[0, k], seeded_block(cot, live, at_block(k, bs)), 1, 1))

        scattered(make, perm, c * STEP, gc_t, r0, r1, bs)

    @pl.when(phase == 1)
    def _():
        def make(k, rows):
            here = at_block(k, bs)
            ap = rows[...].astype(BF16)
            ap_t[here, :] = ap
            _, slope = gelu_parts(dot(fac_a[0, k], ap, 0, 0))
            gh = dot(fac_b[0, k], gc_t[at_block(c * STEP + k, bs), :].astype(BF16), 1, 0)
            return rounded(dot(fac_a[0, k], (gh * slope).astype(BF16), 1, 0))

        gathered_scattered(make, perm, c * STEP, a_t, ga_t, r0, r1, r2, r3, bs)

    @pl.when(phase == 2)
    def _():
        def one(k, u):
            cols = at_block(c * STEP + k, bs)
            value = dot(ga_t[cols, :].astype(BF16), fac_a[0, k], 0, 1)
            gn[:, cols] = value
            acc[...] += value * gamma[:, cols] * zed_block(x, scale, cols)

        each_block(one)

    @pl.when(jnp.logical_and(phase == 2, c == pl.num_programs(1) - 1))
    def _():
        mean = jnp.sum(acc[...], axis=1, keepdims=True) / x.shape[1]
        acc[...] = jnp.broadcast_to(mean, acc.shape)

    def emit(out):
        def one(k, u):
            here = at_block(k, bs)
            cols = at_block(c * STEP + k, bs)
            z = zed_block(x, scale, cols)
            out[:, here] = gradient(seeded_block(cot, live, here), gn[:, cols], gamma[:, cols], z, scale, acc)

        each_block(one, unroll=4)

    last = pl.num_programs(1) - 1
    pl.when(jnp.logical_and(phase == 3, c < last))(lambda: emit(grad_a))
    pl.when(jnp.logical_and(phase == 3, c == last))(lambda: emit(grad_b))


def forward_second(perm, ap_t, fac_one, fac_two, cp_t, c_t, rows):
    phase, c = pl.program_id(0), pl.program_id(1)
    bs = fac_two.shape[2]

    @pl.when(phase == 0)
    def _():
        def one(k, u):
            h, _ = gelu_parts(dot(fac_one[0, k], ap_t[at_block(k, bs), :], 0, 0))
            c_t[at_block(c * STEP + k, bs), :] = rounded(dot(fac_two[0, k], h, 0, 0))

        each_block(one)

    @pl.when(phase == 1)
    def _():
        def one(k, u):
            gather_rows(perm, (c * STEP + k) * bs, c_t, rows.at[u], bs)
            cp_t[at_block(k, bs), :] = rows[u].astype(BF16)

        each_block(one)


def each_split(flags, own, body):
    for k in range(STEP // 2):
        group, within = divmod(k, own)
        base = group * 2 * own + within
        body(0, k, base + flags[0] * own)
        body(1, k, base + (1 - flags[0]) * own)


def back_three(own, skipped, perm, flags, cot, live, moved, cp_t, fac, *refs):
    if len(refs) > 6:
        _, _, _, gc_in, keep, send, gy_out, gc_out, gc_t, even, odd = refs
        gc_t[...] = gc_in[...]
    else:
        keep, send, gy_out, gc_t, even, odd = refs
        gc_out = None
    bs = fac.shape[2]
    outs = (keep, send)

    def make(k):
        here = at_block(k, bs)
        gy = jnp.where(flags[1] == 1, seeded_block(cot, live, here), moved[:, here])
        gy_out[:, here] = gy
        return rounded(dot(fac[0, k], gy, 1, 1))

    def grads(goes, k, block):
        at = at_block(block, bs)
        outs[goes][k] = dot(cp_t[at, :], gy_out[:, at], 1, 0).astype(BF16)

    scattered(make, perm, (pl.program_id(0) + skipped) * STEP, gc_t, even, odd, bs)
    each_split(flags, own, grads)
    if gc_out is not None:
        gc_out[...] = gc_t[...].astype(BF16)


def back_two_one(
    own, perm, flags, gc_t, ap_t, fac_two, fac_one, keep_two, send_two, keep_one, send_one, ga_out, ga_t, h_t, gpre_t, even, odd
):
    c = pl.program_id(0)
    bs = fac_two.shape[2]
    twos, ones = (keep_two, send_two), (keep_one, send_one)

    def make(k):
        here = at_block(k, bs)
        h_t[here, :], slope = gelu_parts(dot(fac_one[0, k], ap_t[here, :], 0, 0))
        gpre = (dot(fac_two[0, k], gc_t[here, :], 1, 0) * slope).astype(BF16)
        gpre_t[here, :] = gpre
        return rounded(dot(fac_one[0, k], gpre, 1, 0))

    def grads(goes, k, block):
        at = at_block(block, bs)
        twos[goes][k] = dot(h_t[at, :], gc_t[at, :], 1, 1).astype(BF16)
        ones[goes][k] = dot(ap_t[at, :], gpre_t[at, :], 1, 1).astype(BF16)

    scattered(make, perm, c * STEP, ga_t, even, odd, bs)
    each_split(flags, own, grads)

    @pl.when(c == pl.num_programs(0) - 1)
    def _():
        ga_out[...] = ga_t[...].astype(BF16)


def back_zero(own, flags, ga_t, gy, x, scale, gamma, fac, keep, send, grad_x, gn, acc):
    phase, c = pl.program_id(0), pl.program_id(1)
    bs = fac.shape[2]
    outs = (keep, send)

    @pl.when(jnp.logical_and(phase == 0, c == 0))
    def _():
        acc[...] = jnp.zeros(acc.shape, F32)

    @pl.when(phase == 0)
    def _():
        def one(goes, k, block):
            at = at_block(block, bs)
            z = zed_block(x, scale, at)
            zg = z * gamma[:, at]
            outs[goes][k, pl.ds(0, bs), :] = dot(zg.astype(BF16), ga_t[at, :], 0, 1).astype(BF16)
            value = dot(ga_t[at, :], fac[0, block], 0, 1)
            gn[:, at_block(c * STEP + block, bs)] = value
            total = jnp.sum(value * z, axis=0, keepdims=True)
            outs[goes][k, pl.ds(bs, EXTRA), :] = jnp.broadcast_to(total, (EXTRA, bs)).astype(BF16)
            acc[...] += value * zg

        each_split(flags, own, one)

    @pl.when(jnp.logical_and(phase == 0, c == pl.num_programs(1) - 1))
    def _():
        mean = jnp.sum(acc[...], axis=1, keepdims=True) / gn.shape[1]
        acc[...] = jnp.broadcast_to(mean, acc.shape)

    @pl.when(phase == 1)
    def _():
        for k in range(STEP):
            cols = at_block(k, bs)
            z = zed_block(x, scale, cols)
            grad_x[:, cols] = gradient(gy[:, cols], gn[:, at_block(c * STEP + k, bs)], gamma[:, cols], z, scale, acc)


class Halving:
    def __init__(self, keep, send, order, own, me, replicas):
        self.keep, self.send, self.order = keep, send, list(order)
        self.left = list(range(replicas.bit_length() - 1))[::-1]
        self.left.remove(self.order[0])
        self.own, self.me, self.replicas = own, me, replicas
        self.came = None

    def go(self):
        bit = self.order.pop(0)
        self.came = lax.ppermute(self.send, "dp", [(i, i ^ (1 << bit)) for i in range(self.replicas)])
        return self

    def add(self):
        if not self.order:
            self.keep, self.send, self.came = self.keep.astype(F32) + self.came.astype(F32), None, None
            return self
        bit = self.order[0]
        place = self.left.index(bit)
        shape = (2**place, 2, 2 ** (len(self.left) - 1 - place) * self.own) + self.keep.shape[1:]
        mine = (self.me >> bit) & 1
        keep, came = self.keep.reshape(shape), self.came.reshape(shape)

        def part(which):
            a = lax.dynamic_index_in_dim(keep, which, 1, keepdims=False)
            b = lax.dynamic_index_in_dim(came, which, 1, keepdims=False)
            total = (a.astype(F32) + b.astype(F32)).astype(self.keep.dtype)
            return total.reshape((shape[0] * shape[2],) + shape[3:])

        self.left.remove(bit)
        self.send, self.keep = part(1 - mine), part(mine)
        self.came = None
        return self

    def finish(self):
        if self.came is not None:
            self.add()
        while self.order:
            self.go().add()
        return self.keep / self.replicas


def met(*halvings, then):
    state = [(h.keep, h.send if h.came is None else h.came) for h in halvings]
    state, then = lax.optimization_barrier((state, then))
    for h, (keep, rest) in zip(halvings, state):
        h.keep = keep
        if h.came is None:
            h.send = rest
        else:
            h.came = rest
    return then


def behind(first, *others):
    state = [(h.keep, h.came) for h in others]
    first.keep, state = lax.optimization_barrier((first.keep, state))
    for h, (keep, came) in zip(others, state):
        h.keep, h.came = keep, came


def on_device(replicas, sections, activations, cotangent, token_ids, gains, factors, monarch_perm):
    x = activations[0]
    gamma = gains
    fac = factors[0]
    perm = monarch_perm[0]
    tokens, width = x.shape
    blocks, bs = fac.shape[1], fac.shape[2]
    own = blocks // replicas
    steps = blocks // STEP
    here = lax.axis_index("section")
    me = lax.axis_index("dp")
    live = jnp.broadcast_to((token_ids != 0).astype(F32)[:, None], (tokens, bs))
    flags = jnp.stack([me & 1, (here == sections - 1).astype(jnp.int32)])
    bits = list(range(replicas.bit_length() - 1))
    other = bits[:1] + bits[2:3] + bits[1:2] + bits[3:]

    tok = whole(tokens, width)
    sca = whole(tokens, bs)
    gam = whole(1, width)
    chunk = (STEP * bs, tokens)
    wide = (tokens, STEP * bs)
    fblock = (1, STEP, bs, bs)
    f_at = lambda which: pl.BlockSpec(fblock, lambda c, *_: (which, c, 0, 0))
    c_at = pl.BlockSpec(chunk, lambda c, *_: (c, 0))
    w_at = pl.BlockSpec(wide, lambda c, *_: (0, c))
    g_at = pl.BlockSpec((1, STEP * bs), lambda c, *_: (0, c))
    feat = lambda dt: jax.ShapeDtypeStruct((width, tokens), dt)
    row = lambda dt: jax.ShapeDtypeStruct((tokens, width), dt)
    small = jax.ShapeDtypeStruct((tokens, bs), F32)
    half = lambda n=0, lead=(): jax.ShapeDtypeStruct(lead + (blocks // 2, bs + n, bs), BF16)
    half_at = pl.BlockSpec((STEP // 2, bs, bs), lambda c, *_: (c, 0, 0))
    more_at = pl.BlockSpec((STEP // 2, bs + EXTRA, bs), lambda c, *_: (c, 0, 0))
    two_at = pl.BlockSpec((2, STEP // 2, bs, bs), lambda c, *_: (0, c, 0, 0))
    big = pltpu.VMEM((width, tokens), F32)
    rows = pltpu.VMEM((UNROLL, bs, tokens), F32)
    block = pltpu.VMEM((bs, tokens), F32)
    part_t = pltpu.VMEM(chunk, BF16)
    part = (steps - 1) * STEP * bs
    last = steps - 1

    def phased(*picks):
        def at(ph, c):
            out = c if picks[-1] is None else picks[-1]
            for i in range(len(picks) - 2, -1, -1):
                out = jnp.where(ph == i, c if picks[i] is None else picks[i], out)
            return out

        return at

    pick = lambda values: lambda ph: jnp.where(ph == 0, values[0], jnp.where(ph == 1, values[1], values[2]))
    a_which, a_at = pick((0, 1, 0)), phased(None, None, None, last)
    b_which, b_at = pick((3, 2, 2)), phased(None, None, last, last)
    cot_at, out_at, mid_at = phased(None, last, last, None), phased(0, 0, 0, None), phased(0, None, last, last)
    mid = pl.BlockSpec(chunk, lambda ph, c, *_: (mid_at(ph, c), 0))
    ap_t, scale, *grad_x = call(
        first_pass,
        "first_pass",
        (4, steps),
        [
            tok,
            pl.BlockSpec(wide, lambda ph, c, *_: (0, cot_at(ph, c))),
            sca,
            gam,
            pl.BlockSpec(fblock, lambda ph, c, *_: (a_which(ph), a_at(ph, c), 0, 0)),
            pl.BlockSpec(fblock, lambda ph, c, *_: (b_which(ph), b_at(ph, c), 0, 0)),
        ],
        [mid, sca, pl.BlockSpec(wide, lambda ph, c, *_: (0, jnp.minimum(out_at(ph, c), last - 1))), whole(*wide)],
        [
            feat(BF16),
            small,
            jax.ShapeDtypeStruct((tokens, part), BF16),
            jax.ShapeDtypeStruct(wide, BF16),
        ],
        [big, big, big, pltpu.VMEM((tokens, width), F32), pltpu.VMEM((tokens, bs), F32)] + [block] * 4,
        vmem=60,
    )(perm, x, cotangent, live, gamma, fac, fac)
    moved = [lax.ppermute(piece, "section", [(i, i - 1) for i in range(1, sections)]) for piece in grad_x]

    early, rest = phased(None, last), phased(0, None)
    cp_t = call(
        forward_second,
        "forward_second",
        (2, steps),
        [
            pl.BlockSpec(chunk, lambda ph, c, *_: (early(ph, c), 0)),
            pl.BlockSpec(fblock, lambda ph, c, *_: (1, early(ph, c), 0, 0)),
            pl.BlockSpec(fblock, lambda ph, c, *_: (2, early(ph, c), 0, 0)),
        ],
        pl.BlockSpec(chunk, lambda ph, c, *_: (rest(ph, c), 0)),
        feat(BF16),
        [big, rows],
    )(perm, ap_t, fac, fac)

    start = lambda keep, send, order: Halving(keep, send, order, own, me, replicas)
    shapes = [half(), half(), row(BF16), feat(F32)]
    scratch = [block, block]
    partial = call(
        functools.partial(back_three, own, 0),
        "back_three_early",
        (steps - 1,),
        [w_at, sca, w_at, c_at, f_at(3)],
        [half_at, half_at, w_at, whole(width, tokens)],
        shapes,
        scratch,
        prefetch=2,
    )(perm, flags, cotangent, live, moved[0], cp_t, fac)
    shift = lambda spec: pl.BlockSpec(spec.block_shape, lambda c, *_: spec.index_map(c + last))
    held = pl.BlockSpec(memory_space=pl.ANY)
    partial, moved[1] = lax.optimization_barrier((partial, moved[1]))
    keep, send, gy, gc_t = call(
        functools.partial(back_three, own, steps - 1),
        "back_three_late",
        (1,),
        [shift(w_at), sca, w_at, shift(c_at), shift(f_at(3)), held, held, held, whole(width, tokens)],
        [shift(half_at), shift(half_at), shift(w_at), whole(width, tokens)],
        shapes[:3] + [feat(BF16)],
        [big] + scratch,
        prefetch=2,
        aliases={7: 0, 8: 1, 9: 2},
    )(perm, flags, cotangent, live, moved[1], cp_t, fac, *partial)
    three = start(keep, send, bits)
    three.go()
    keep_two, send_two, keep_one, send_one, ga_t = call(
        functools.partial(back_two_one, own),
        "back_two_one",
        (steps,),
        [c_at, c_at, f_at(2), f_at(1)],
        [half_at] * 4 + [whole(width, tokens)],
        [half()] * 4 + [feat(BF16)],
        [big, part_t, part_t, block, block],
        prefetch=2,
    )(perm, flags, gc_t, ap_t, fac, fac)
    two, one = start(keep_two, send_two, other), start(keep_one, send_one, bits)
    ga_t, one.keep, one.send, two.keep, two.send = met(three, then=[ga_t, one.keep, one.send, two.keep, two.send])
    three.add()
    (ga_t,) = met(three, then=[ga_t])
    one.go()
    two.go()
    three.go()
    held_at = lambda shape, at, *lead: pl.BlockSpec(shape, lambda ph, c, *_: lead + (at(ph, c),) + (0,) * (len(shape) - 1 - len(lead)))
    across = lambda shape, at: pl.BlockSpec(shape, lambda ph, c, *_: (0, at(ph, c)))
    both = phased(None, None)
    keep_zero, send_zero, out_grad = call(
        functools.partial(back_zero, own),
        "back_zero",
        (2, steps),
        [
            held_at(chunk, early),
            across(wide, rest),
            across(wide, both),
            sca,
            across((1, STEP * bs), both),
            held_at(fblock, early, 0),
        ],
        [held_at(more_at.block_shape, early)] * 2 + [across(wide, rest)],
        [half(EXTRA), half(EXTRA), row(BF16)],
        [pltpu.VMEM((tokens, width), F32), pltpu.VMEM((tokens, bs), F32)],
    )(flags, ga_t, gy, x, scale, gamma, fac)
    zero = start(keep_zero, send_zero, bits)
    out_grad, zero.keep, zero.send = met(one, two, three, then=[out_grad, zero.keep, zero.send])
    zero.go()
    one.add().go()
    zero.add().go()
    three.add().go()
    behind(three, two)
    two.add().go()
    one.add().go()
    zero.add().go()
    behind(zero, one, two)
    total = [each.finish() for each in (zero, one, two, three)]
    grad_gamma = total[0][:, bs, :].reshape(1, own * bs)
    total[0] = total[0][:, :bs, :]
    return (out_grad[None], jnp.stack(total)[None], grad_gamma)


def solution(mesh):
    replicas, sections = mesh.shape["dp"], mesh.shape["section"]
    in_specs = (
        P("section", "dp", None),
        P("dp", None),
        P("dp"),
        P("section", None),
        P("section", None, None, None, None),
        P("section", None),
    )
    out_specs = (P("section", "dp", None), P("section", None, "dp", None, None), P("section", "dp"))
    return jax.shard_map(
        functools.partial(on_device, replicas, sections),
        mesh=mesh,
        in_specs=in_specs,
        out_specs=out_specs,
        check_vma=False,
    )
```
